256 devices in a mesh: samples: 32 (over y, x, core), cols: 8 (over z).
Axes of the slice: x: 4, y: 4, z: 8, core: 2. Of those that a mesh axis runs over, the one named last changes fastest.
Arguments:
- features: bfloat16 [131072, 440], P('samples'), may hold values from -6 to 6
- labels: int32 [131072], P('samples'), may hold values from 0 to 146
- weights: float32 [131072, 147], P('samples'), may hold values from -6 to 6
- block_order: int32 [32], replicated, may hold values from 0 to 31, each once
- block_starts: int32 [32], replicated, may hold values from 0 to 3968
- inverses: float32 [4, 4096, 4096], P(None, 'samples', 'cols'), may hold values from -0.125 to 1.5
Outputs:
- new_weights: float32 [131072, 147], P('samples')
The draws below stay inside these ranges and needn't reach their ends.
All inputs are finite; a program needn't handle non-finite values.
Results may differ from the reference program's by a relative error of at most 0.0005.
Values may be sent and summed in bfloat16 or wider, within the bound.
A program may use at most 128 MiB of HBM per device.

```python
import math
import jax
import jax.numpy as jnp
from jax import lax

F = 440
C = 147
B = 4096
NUPD = 4
ROWS_DEV = 4096
N = 131072
NBLK = 32
RB = 128
QI = 16
CB = 512
N_SAMPLES = 32


def draw_features(key, part):
    clusters = 32
    first, second, third = jax.random.split(jax.random.fold_in(key, 11), 3)
    member = jax.random.randint(second, (N,), 0, clusters)
    centers = jax.random.normal(first, (clusters, F), jnp.float32) * 1.5 ** 0.5
    spread = jax.random.normal(third, (N, F), jnp.float32) * 0.5 ** 0.5
    values = jnp.take(centers, member, axis=0) + spread
    return jnp.clip(values, -6.0, 6.0).astype(jnp.bfloat16)


def draw_inverses(key, part):

    def single(subkey):
        first, second = jax.random.split(subkey)
        diagonal = jax.random.uniform(first, (B,), jnp.float32, 0.5, 1.5)
        spread = jax.random.truncated_normal(second, -4.0, 4.0, (B, B), jnp.float32) * (0.5 / B ** 0.5)
        unit = jnp.eye(B, dtype=jnp.float32)
        square = spread * (1.0 - unit) + unit * diagonal[None, :]
        index = jnp.arange(B, dtype=jnp.int32)
        groups = RB // QI
        group = index // (B // groups)
        owner = index % (B // groups) // QI
        inner = index % QI
        source = (owner * RB + group * QI + inner).astype(jnp.int32)
        return square[:, source]
    return jax.lax.map(single, jax.random.split(jax.random.fold_in(key, 7), NUPD))


def plant(drawn, key, least, top_value):
    spot = [jax.random.randint(jax.random.fold_in(key, axis), (), 0, length) for axis, length in enumerate(drawn.shape)]
    widest = drawn.shape.index(max(drawn.shape))
    neighbour = spot[:widest] + [(spot[widest] + 1) % drawn.shape[widest]] + spot[widest + 1:]
    return drawn.at[tuple(spot)].set(least).at[tuple(neighbour)].set(top_value)


def block_scale(rng, dims, pieces, low, high):
    def one(axis_at, parts):
        draws = jax.random.uniform(jax.random.fold_in(jax.random.fold_in(rng, 6), axis_at), (parts,), jnp.float32, low / len(pieces), high / len(pieces))
        return jnp.repeat(jnp.exp(draws), dims[axis_at] // parts).reshape((-1,) + (1,) * (len(dims) - axis_at - 1))

    level = one(*pieces[0])
    for cut in pieces[1:]:
        level = level * one(*cut)
    return level


def noise(key, extent, scale, bound, cuts=(), kind=jnp.bfloat16):
    factor_of = block_scale(key, extent, cuts, -0.22, 0.18) if cuts else 1.0
    drawn = jax.random.normal(key, extent, jnp.float32) * scale * factor_of
    return jnp.minimum(jnp.maximum(drawn, -bound), bound).astype(kind)


def setup_inputs(seed: int = 0) -> dict:
    key_of = jax.random.split(jax.random.key(seed), 7)
    return {
        "features": draw_features(jax.random.fold_in(key_of[6], 71), 0),
        "labels": plant(jax.random.randint(key_of[1], (N,), 0, C), jax.random.fold_in(key_of[1], 1), 0, C - 1).astype(jnp.int32),
        "weights": noise(key_of[2], (N, C), 1.0, 6.0, ((0, 32),), jnp.float32),
        "block_order": jax.random.permutation(key_of[3], NBLK).astype(jnp.int32),
        "block_starts": plant(jax.random.randint(key_of[4], (NBLK,), 0, ROWS_DEV - RB + 1), jax.random.fold_in(key_of[4], 1), 0, ROWS_DEV - RB).astype(jnp.int32),
        "inverses": draw_inverses(jax.random.fold_in(key_of[6], 71), 0),
    }


RIDGE = 0.5

def member_rows(start):
    shard = jnp.arange(N_SAMPLES, dtype=jnp.int32)
    slot = jnp.arange(RB, dtype=jnp.int32)
    rows_r = (shard[:, None] * ROWS_DEV + start + slot[None, :]).reshape(-1).astype(jnp.int32)
    index = jnp.arange(B, dtype=jnp.int32)
    group = index // CB
    owner = index % CB // QI
    inner = index % QI
    rows_q = (owner * ROWS_DEV + start + group * QI + inner).astype(jnp.int32)
    return (rows_r, rows_q)

def block_products(features, current, rows_q):
    chosen = features[rows_q].astype(jnp.float32)
    chosen_norms = lax.optimization_barrier(jnp.sum(chosen * chosen, axis=1))
    shaped_x = features.reshape(N_SAMPLES, ROWS_DEV, F)
    shaped_w = current.reshape(N_SAMPLES, ROWS_DEV, C)

    def accumulate(total, pair):
        block_x, block_w = pair
        values = block_x.astype(jnp.float32)
        inner = jnp.dot(values, chosen.T, precision=lax.Precision.HIGHEST)
        norms = lax.optimization_barrier(jnp.sum(values * values, axis=1))
        panel = jnp.exp((2.0 * inner - norms[:, None] - chosen_norms[None, :]) / F)
        return (total + jnp.dot(panel.T, block_w, precision=lax.Precision.HIGHEST), None)
    total, unused = lax.scan(accumulate, jnp.zeros((B, C), jnp.float32), (shaped_x, shaped_w))
    return total

def reference(features, labels, weights, block_order, block_starts, inverses):
    current = weights
    scale = 1.0 / math.sqrt(N)
    classes = jnp.arange(C, dtype=jnp.int32)
    for step in range(NUPD):
        start = block_starts[block_order[step]]
        rows_r, rows_q = member_rows(start)
        products = block_products(features, current, rows_q)
        onehot = (labels[rows_q][:, None] == classes[None, :]).astype(jnp.float32)
        residual = onehot - scale * products - RIDGE * current[rows_q]
        delta = jnp.dot(inverses[step], residual, precision=lax.Precision.HIGHEST)
        current = current.at[rows_r].add(delta)
    return current
```

```python
import math

import jax
import jax.numpy as jnp
from jax import lax
from jax.experimental import pallas as pl
from jax.experimental.pallas import tpu as pltpu
from jax.sharding import Mesh
from jax.sharding import PartitionSpec as P

SAMPLES = ("sy", "sx", "sc")
MESH = pl.DeviceIdType.MESH
RIDGE = 0.5
UPD = 4
CHIPS = 16
COLS = 8
SPAN = 128
PIECE = 16
GROUP = 512
WIDTH = 440
DEPTH = 448
LANES = 128
ROWS = 4096
NBLOCK = 1024
JBLOCK = 256
EARLIER = [(early, late) for late in range(UPD) for early in range(late)]
VMEM = pl.BlockSpec(memory_space=pltpu.VMEM)
SMEM = pl.BlockSpec(memory_space=pltpu.SMEM)
ANY = pl.BlockSpec(memory_space=pl.ANY)


def where_am_i():
    return (
        lax.axis_index("sy"),
        lax.axis_index("sx"),
        lax.axis_index("sc"),
        lax.axis_index("cols"),
    )


def push(src, dst, send, recv, device):
    pltpu.make_async_remote_copy(
        src_ref=src,
        dst_ref=dst,
        send_sem=send,
        recv_sem=recv,
        device_id=device,
        device_id_type=MESH,
    ).start()


def drain(ref, sem):
    pltpu.make_async_copy(ref, ref, sem).wait()


def gather_kernel(memb, fb, inv, term, a_out, fb_sib, inv_sib, o_out, send, recv, psend, precv, local):
    y, x, c, z = where_am_i()
    sib = (y, x, 1 - c, z)

    def at(first, second):
        down = c * first + (1 - c) * second
        over = (1 - c) * first + c * second
        return lax.rem(y + down, 4), lax.rem(x + over, 4)

    def shard_of(first, second):
        row, col = at(first, second)
        return (row * 4 + col) * 2 + c

    barrier = pltpu.get_barrier_semaphore()
    pl.semaphore_signal(barrier, inc=1, device_id=sib, device_id_type=MESH)
    for step in range(1, 4):
        for where in ((step, 0), (0, step)):
            row, col = at(*where)
            pl.semaphore_signal(barrier, inc=1, device_id=(row, col, c, z), device_id_type=MESH)
    pl.semaphore_wait(barrier, 7)

    me = shard_of(0, 0)
    own = pltpu.make_async_copy(memb, a_out.at[:, me], local.at[0])
    own.start()
    kept = pltpu.make_async_copy(term.at[c], o_out.at[:, c], local.at[1])
    kept.start()

    def block(shard):
        return a_out.at[:, shard]

    for step in (1, 3, 2):
        row, col = at(step, 0)
        push(memb, block(me), send, recv.at[me], (row, col, c, z))
    for step in (1, 3, 2):
        row, col = at(0, step)
        push(memb, block(me), send, recv.at[me], (row, col, c, z))
    push(memb, block(me), send, recv.at[me], sib)
    pair = (
        (term.at[1 - c], o_out.at[:, c]),
        (fb, fb_sib),
        (inv, inv_sib),
    )
    for number, (src, dst) in enumerate(pair):
        push(src, dst, psend.at[number], precv.at[number], sib)
    for step in (3, 1, 2):
        source = shard_of(step, 0)
        drain(block(source), recv.at[source])
        for other in (1, 3, 2):
            row, col = at(0, other)
            push(block(source), block(source), send, recv.at[source], (row, col, c, z))
        push(block(source), block(source), send, recv.at[source], sib)
    for first in (0, 3, 1, 2):
        for second in (3, 1, 2):
            source = shard_of(first, second)
            drain(block(source), recv.at[source])
            push(block(source), block(source), send, recv.at[source], sib)
    for chip in range(CHIPS):
        source = chip * 2 + 1 - c
        drain(block(source), recv.at[source])
    own.wait()
    kept.wait()
    for number, (src, dst) in enumerate(pair):
        drain(dst, precv.at[number])
        drain(src, psend.at[number])
    drain(a_out.at[:, pl.ds(0, 31)], send)


def gather(memb, fb, inv, term):
    return pl.pallas_call(
        gather_kernel,
        out_shape=(
            jax.ShapeDtypeStruct((UPD, 2 * CHIPS, PIECE, DEPTH), jnp.bfloat16),
            jax.ShapeDtypeStruct(fb.shape, fb.dtype),
            jax.ShapeDtypeStruct(inv.shape, inv.dtype),
            jax.ShapeDtypeStruct((UPD, 2, PIECE, LANES), jnp.float32),
        ),
        in_specs=[VMEM, VMEM, ANY, VMEM],
        out_specs=[VMEM, VMEM, ANY, VMEM],
        scratch_shapes=[
            pltpu.SemaphoreType.DMA,
            pltpu.SemaphoreType.DMA((2 * CHIPS,)),
            pltpu.SemaphoreType.DMA((3,)),
            pltpu.SemaphoreType.DMA((3,)),
            pltpu.SemaphoreType.DMA((2,)),
        ],
        compiler_params=pltpu.CompilerParams(
            collective_id=0, has_side_effects=True, vmem_limit_bytes=24 << 20
        ),
        name="gather_members",
    )(memb, fb, inv, term)


def split3(value):
    high = value.astype(jnp.bfloat16).astype(jnp.float32)
    rest = value - high
    middle = rest.astype(jnp.bfloat16).astype(jnp.float32)
    return high, middle, rest - middle


def kernel_values(exponent):
    return jnp.exp2(exponent * (math.log2(math.e) / WIDTH)).astype(jnp.bfloat16)


def panel_kernel(ft, wt, a, fb_own, fb_sib, p_out, m_out, acc, fa, wf):
    step = pl.program_id(0)
    c = lax.axis_index("sc")

    @pl.when(step == 0)
    def _():
        acc[...] = jnp.zeros_like(acc)
        wf[...] = jnp.zeros_like(wf)

    features = ft[...]
    norm = jnp.sum(jnp.square(features.astype(jnp.float32)), axis=0, keepdims=True)
    parts = split3(norm)
    line = lax.broadcasted_iota(jnp.int32, (8, NBLOCK), 0)
    extra = jnp.where(line < 6, 1.0, 0.0)
    for number, part in enumerate(parts):
        extra = jnp.where(line == number, -part, extra)
    fa[0:432, :] = ft[0:432, :]
    tail = ft[432:440, :].astype(jnp.float32)
    fa[432:448, :] = jnp.concatenate([tail, extra], axis=0).astype(jnp.bfloat16)
    wf[0:147, :] = wt[...]
    w = wf[...].astype(jnp.bfloat16)

    def body(block, carry):
        rows = pl.ds(pl.multiple_of(block * JBLOCK, JBLOCK), JBLOCK)
        exponent = jnp.dot(a[rows, :], fa[...], preferred_element_type=jnp.float32)
        acc[rows, :] += lax.dot_general(
            kernel_values(exponent),
            w,
            (((1,), (1,)), ((), ())),
            preferred_element_type=jnp.float32,
        )
        return carry

    lax.fori_loop(0, UPD * GROUP // JBLOCK, body, 0)

    @pl.when(step == pl.num_programs(0) - 1)
    def _():
        for half in range(2):
            p_out[half] = acc[:, half * LANES : (half + 1) * LANES].astype(jnp.bfloat16)
        for number, (early, late) in enumerate(EARLIER):
            lines = a[late * GROUP : (late + 1) * GROUP, :]
            for fb, place in ((fb_own, c), (fb_sib, 1 - c)):
                exponent = jnp.dot(lines, fb[early], preferred_element_type=jnp.float32)
                m_out[number, place] = kernel_values(exponent)


def panel(ft, wt, a, fb_own, fb_sib):
    total = UPD * GROUP
    whole = lambda *shape: pl.BlockSpec(shape, lambda n: (0,) * len(shape))
    return pl.pallas_call(
        panel_kernel,
        grid=(ROWS // NBLOCK,),
        out_shape=(
            jax.ShapeDtypeStruct((2, total, LANES), jnp.bfloat16),
            jax.ShapeDtypeStruct((len(EARLIER), 2, GROUP, SPAN), jnp.bfloat16),
        ),
        in_specs=[
            pl.BlockSpec((WIDTH, NBLOCK), lambda n: (0, n)),
            pl.BlockSpec((147, NBLOCK), lambda n: (0, n)),
            whole(total, DEPTH),
            whole(UPD - 1, DEPTH, SPAN),
            whole(UPD - 1, DEPTH, SPAN),
        ],
        out_specs=[whole(2, total, LANES), whole(len(EARLIER), 2, GROUP, SPAN)],
        scratch_shapes=[
            pltpu.VMEM((total, 2 * LANES), jnp.float32),
            pltpu.VMEM((DEPTH, NBLOCK), jnp.bfloat16),
            pltpu.VMEM((2 * LANES, NBLOCK), jnp.float32),
        ],
        compiler_params=pltpu.CompilerParams(vmem_limit_bytes=40 << 20),
        name="panel_products",
    )(ft, wt, a, fb_own, fb_sib)


def chain_kernel(
    p, o, inv_own, inv_sib, m, starts, out,
    got_p, r0, r_send, r_full, d_part, d_got, d_own, h_own, h_full, c_part, c_got, high, low,
    send, recv,
):
    y, x, c, z = where_am_i()
    chip = y * 4 + x
    shard = chip * 2 + c
    scale = 1.0 / math.sqrt(ROWS * 32)
    SP, SPR, SR, SD, SH, SX, SC = 0, 1, 2, 6, 10, 14, 18

    def peer(offset):
        row = lax.rem(y + offset // 4, 4)
        col = lax.rem(x + lax.rem(offset, 4), 4)
        return row, col, row * 4 + col

    def over(low_end, high_end, body):
        def step(index, carry):
            body(index)
            return carry

        lax.fori_loop(low_end, high_end, step, 0)

    barrier = pltpu.get_barrier_semaphore()

    def greet_plane(offset):
        row, col, _ = peer(offset)
        for core in range(2):

            @pl.when((offset > 0) | (core != c))
            def _():
                pl.semaphore_signal(
                    barrier, inc=1, device_id=(row, col, core, z), device_id_type=MESH
                )

    def greet_column(offset):
        for core in range(2):
            pl.semaphore_signal(
                barrier, inc=1, device_id=(y, x, core, lax.rem(z + offset, COLS)), device_id_type=MESH
            )

    over(0, CHIPS, greet_plane)
    over(1, COLS, greet_column)
    pl.semaphore_wait(barrier, 31 + 14)

    def send_products(first, count, number):
        def body(offset):
            row, col, other = peer(offset)
            for core in range(2):

                @pl.when((offset > 0) | (core != c))
                def _():
                    push(
                        p.at[core, pl.ds(first, count), other],
                        got_p.at[pl.ds(first, count), shard],
                        send.at[number],
                        recv.at[number],
                        (row, col, core, z),
                    )

        over(0, CHIPS, body)

    def sums_of_products(first, count, number):
        drain(got_p.at[pl.ds(first, count), pl.ds(0, 31)], recv.at[number])
        for t in range(first, first + count):
            got_p[t, shard] = p[c, t, chip]
            r0[t] = o[t] - scale * jnp.sum(got_p[t].astype(jnp.float32), axis=0)

    def send_residual(t):
        def body(offset):
            row, col, _ = peer(offset)
            push(r_send.at[t], r_full.at[t, chip], send.at[SR + t], recv.at[SR + t], (row, col, c, z))

        over(1, CHIPS, body)
        r_full[t, chip] = r_send[t]

    send_products(0, 1, SP)
    for t in range(UPD):
        for inv, place in ((inv_own, c), (inv_sib, 1 - c)):
            value = inv[t]
            top = value.astype(jnp.bfloat16)
            high[t, place] = top
            low[t, place] = (value - top.astype(jnp.float32)).astype(jnp.bfloat16)
    sums_of_products(0, 1, SP)
    r_send[0] = r0[0]
    send_residual(0)
    send_products(1, 3, SPR)

    base = None
    for t in range(UPD):
        drain(r_full.at[t, pl.ds(0, 15)], recv.at[SR + t])
        residual = r_full[t].reshape(GROUP, LANES)
        top = residual.astype(jnp.bfloat16)
        rest = (residual - top.astype(jnp.float32)).astype(jnp.bfloat16)
        for half in range(2):
            value = jnp.dot(high[t, half], top, preferred_element_type=jnp.float32)
            value += jnp.dot(high[t, half], rest, preferred_element_type=jnp.float32)
            value += jnp.dot(low[t, half], top, preferred_element_type=jnp.float32)
            d_part[t, pl.ds(half * 4, 4)] = value.reshape(4, 32, LANES)

        def send_partial(offset):
            other = lax.rem(z + offset, COLS)
            push(d_part.at[t, other], d_got.at[t, z], send.at[SD + t], recv.at[SD + t], (y, x, c, other))

        over(1, COLS, send_partial)
        d_got[t, z] = d_part[t, z]
        drain(d_got.at[t, pl.ds(0, 7)], recv.at[SD + t])
        delta = jnp.sum(d_got[t], axis=0)
        d_own[t] = delta
        if t < UPD - 1:
            h_own[t] = delta.astype(jnp.bfloat16)

            def send_high(offset):
                other = lax.rem(z + offset, COLS)
                push(h_own.at[t], h_full.at[t, z], send.at[SH + t], recv.at[SH + t], (y, x, c, other))

            over(1, COLS, send_high)
            h_full[t, z] = h_own[t]
        keeper = z // 4
        place = pl.ds(pl.multiple_of(lax.rem(z, 4) * 32, 32), 32)

        def send_result(offset):
            other = lax.rem(z + offset, COLS)

            @pl.when((offset > 0) | (keeper != c))
            def _():
                push(
                    d_own.at[t],
                    out.at[t, c, place],
                    send.at[SX + t],
                    recv.at[SX + t],
                    (y, x, keeper, other),
                )

        over(0, COLS, send_result)

        @pl.when(keeper == c)
        def _():
            out[t, c, place] = d_own[t]

        if t == UPD - 1:
            break
        if t == 0:
            sums_of_products(1, 3, SPR)
        late = t + 1
        partial = None
        for early in range(t):
            for half in range(2):
                term = jnp.dot(
                    m[EARLIER.index((early, late)), half],
                    h_full[early, pl.ds(half * 4, 4)].reshape(SPAN, LANES),
                    preferred_element_type=jnp.float32,
                )
                partial = term if partial is None else partial + term
        drain(h_full.at[t, pl.ds(0, 7)], recv.at[SH + t])
        for half in range(2):
            term = jnp.dot(
                m[EARLIER.index((t, late)), half],
                h_full[t, pl.ds(half * 4, 4)].reshape(SPAN, LANES),
                preferred_element_type=jnp.float32,
            )
            partial = term if partial is None else partial + term
        c_part[t] = partial.astype(jnp.bfloat16).reshape(CHIPS, 32, LANES)

        def send_correction(offset):
            row, col, other = peer(offset)
            push(
                c_part.at[t, other], c_got.at[t, chip], send.at[SC + t], recv.at[SC + t], (row, col, c, z)
            )

        over(1, CHIPS, send_correction)
        c_got[t, chip] = c_part[t, chip]
        line = lax.broadcasted_iota(jnp.int32, (32, 2 * SPAN), 0)
        column = lax.broadcasted_iota(jnp.int32, (32, 2 * SPAN), 1)
        member = starts[late] + z * PIECE + lax.rem(line, PIECE)
        same = line // PIECE == column // SPAN
        shared = jnp.zeros((32, LANES), jnp.float32)
        for early in range(late):
            hit = same & (member == starts[early] + lax.rem(column, SPAN))
            shared += jnp.dot(
                jnp.where(hit, RIDGE, 0.0).astype(jnp.bfloat16),
                h_full[early].reshape(2 * SPAN, LANES),
                preferred_element_type=jnp.float32,
            )
        drain(c_got.at[t, pl.ds(0, 15)], recv.at[SC + t])
        r_send[late] = r0[late] - shared - scale * jnp.sum(c_got[t].astype(jnp.float32), axis=0)
        send_residual(late)

    for t in range(UPD):

        @pl.when(keeper == c)
        def _():
            drain(d_got.at[t, pl.ds(0, 7)], recv.at[SX + t])
            drain(d_got.at[t, pl.ds(0, 7)], send.at[SX + t])

        @pl.when(keeper != c)
        def _():
            drain(d_got.at[t], recv.at[SX + t])
            drain(d_got.at[t], send.at[SX + t])

        drain(r_full.at[t, pl.ds(0, 15)], send.at[SR + t])
        drain(d_got.at[t, pl.ds(0, 7)], send.at[SD + t])
        if t < UPD - 1:
            drain(h_full.at[t, pl.ds(0, 7)], send.at[SH + t])
            drain(c_got.at[t, pl.ds(0, 15)], send.at[SC + t])
    drain(got_p.at[pl.ds(0, 1), pl.ds(0, 31)], send.at[SP])
    drain(got_p.at[pl.ds(1, 3), pl.ds(0, 31)], send.at[SPR])


def chain(p, o, inv_own, inv_sib, m, starts):
    f32, bf16 = jnp.float32, jnp.bfloat16
    return pl.pallas_call(
        chain_kernel,
        out_shape=jax.ShapeDtypeStruct((UPD, 2, SPAN, LANES), f32),
        in_specs=[VMEM] * 5 + [SMEM],
        out_specs=VMEM,
        scratch_shapes=[
            pltpu.VMEM((UPD, 2 * CHIPS, 32, LANES), bf16),
            pltpu.VMEM((UPD, 32, LANES), f32),
            pltpu.VMEM((UPD, 32, LANES), f32),
            pltpu.VMEM((UPD, CHIPS, 32, LANES), f32),
            pltpu.VMEM((UPD, COLS, 32, LANES), f32),
            pltpu.VMEM((UPD, COLS, 32, LANES), f32),
            pltpu.VMEM((UPD, 32, LANES), f32),
            pltpu.VMEM((UPD - 1, 32, LANES), bf16),
            pltpu.VMEM((UPD - 1, COLS, 32, LANES), bf16),
            pltpu.VMEM((UPD - 1, CHIPS, 32, LANES), bf16),
            pltpu.VMEM((UPD - 1, CHIPS, 32, LANES), bf16),
            pltpu.VMEM((UPD, 2, SPAN, GROUP), bf16),
            pltpu.VMEM((UPD, 2, SPAN, GROUP), bf16),
            pltpu.SemaphoreType.DMA((21,)),
            pltpu.SemaphoreType.DMA((21,)),
        ],
        compiler_params=pltpu.CompilerParams(
            collective_id=1, has_side_effects=True, vmem_limit_bytes=40 << 20
        ),
        name="update_chain",
    )(p, o, inv_own, inv_sib, m, starts)


def local(features, labels, weights, block_order, block_starts, inverses):
    c = lax.axis_index("sc")
    group = lax.axis_index("cols")
    classes = weights.shape[1]
    starts = block_starts[block_order[:UPD]]
    ft = features.T
    wt = weights.T

    def window(array, first, size):
        return jnp.stack(
            [lax.dynamic_slice_in_dim(array, starts[t] + first, size, array.ndim - 1) for t in range(UPD)]
        )

    blocks = window(ft, 0, SPAN)
    norms = jnp.sum(jnp.square(blocks.astype(jnp.float32)), axis=1)
    parts = jnp.stack(split3(-norms), axis=1)
    ones = jnp.ones_like(parts)
    gap = jnp.zeros_like(parts[:, :2])
    fb = jnp.concatenate(
        [blocks[:3], jnp.concatenate([parts, ones, gap], axis=1)[:3].astype(jnp.bfloat16)], axis=1
    )
    offset = group * PIECE
    sides = jnp.concatenate(
        [blocks * 2, jnp.concatenate([ones, parts, gap], axis=1).astype(jnp.bfloat16)], axis=1
    )
    memb = jnp.swapaxes(lax.dynamic_slice_in_dim(sides, offset, PIECE, 2), 1, 2)
    member_w = window(wt, offset, PIECE)
    member_l = window(labels, offset, PIECE)
    onehot = (member_l[:, None, :] == jnp.arange(classes, dtype=jnp.int32)[None, :, None]).astype(jnp.float32)
    term = jnp.swapaxes(onehot - RIDGE * member_w, 1, 2)
    term = jnp.pad(term, ((0, 0), (0, 0), (0, 2 * LANES - classes)))
    term = jnp.swapaxes(term.reshape(UPD, PIECE, 2, LANES), 0, 2)
    term = jnp.swapaxes(term, 1, 2)
    a, fb_sib, inv_sib, own = gather(memb, fb, inverses, term)
    p, m = panel(ft, wt, a.reshape(UPD * GROUP, DEPTH), fb, fb_sib)
    deltas = chain(
        p.reshape(2, UPD, CHIPS, 32, LANES),
        own.reshape(UPD, 32, LANES),
        inverses,
        inv_sib,
        m,
        starts,
    )
    current = weights
    for t in range(UPD):
        delta = jnp.concatenate([deltas[t, 0], deltas[t, 1]], axis=1)[:, :classes]
        before = lax.dynamic_slice_in_dim(current, starts[t], SPAN, 0)
        current = lax.dynamic_update_slice_in_dim(current, before + delta, starts[t], 0)
    return current


def solution(mesh):
    finer = Mesh(
        mesh.devices.reshape(4, 4, 2, mesh.shape["cols"]), ("sy", "sx", "sc", "cols")
    )
    in_specs = (P(SAMPLES, None), P(SAMPLES), P(SAMPLES, None), P(), P(), P(None, SAMPLES, "cols"))
    return jax.shard_map(
        local, mesh=finer, in_specs=in_specs, out_specs=P(SAMPLES, None), check_vma=False
    )
```

```python
import math

import jax
import jax.numpy as jnp
from jax import lax
from jax.experimental import pallas as pl
from jax.experimental.pallas import tpu as pltpu
from jax.sharding import Mesh
from jax.sharding import PartitionSpec as P

SAMPLES = ("sy", "sx", "sc")
MESH = pl.DeviceIdType.MESH
HIGHEST = lax.Precision.HIGHEST
RIDGE = 0.5
UPD = 4
BLOCKS = 32
CHIPS = 16
COLS = 8
SPAN = 128
PIECE = 16
GROUP = 512
WIDTH = 440
DEPTH = 512
LANES = 128
CLASSES = 147
ROWS = 4096
NBLOCK = 1024
WINDOW = 256
EARLIER = [(early, late) for late in range(UPD) for early in range(late)]
VMEM = pl.BlockSpec(memory_space=pltpu.VMEM)
SMEM = pl.BlockSpec(memory_space=pltpu.SMEM)
ANY = pl.BlockSpec(memory_space=pl.ANY)
F32, BF16 = jnp.float32, jnp.bfloat16
NT = (((1,), (1,)), ((), ()))


def push(src, dst, send, recv, device):
    pltpu.make_async_remote_copy(
        src_ref=src,
        dst_ref=dst,
        send_sem=send,
        recv_sem=recv,
        device_id=device,
        device_id_type=MESH,
    ).start()


def drain(ref, sem):
    pltpu.make_async_copy(ref, ref, sem).wait()


def over(low, high, body):
    def step(index, carry):
        body(index)
        return carry

    lax.fori_loop(low, high, step, 0)


def iota(shape, dim):
    return lax.broadcasted_iota(jnp.int32, shape, dim)


def dot(a, b):
    return jnp.dot(a, b, preferred_element_type=F32)


def split3(value):
    high = value.astype(BF16).astype(F32)
    rest = value - high
    middle = rest.astype(BF16).astype(F32)
    return high, middle, rest - middle


def kernel_values(exponent):
    return jnp.exp2(exponent * (math.log2(math.e) / WIDTH)).astype(BF16)


def window_of(start):
    base = jnp.minimum(start // LANES, (ROWS - WINDOW) // LANES) * LANES
    return pl.multiple_of(base, LANES), start - base


MEM, MEM_REST, SIB, SIB_REST, TERM, FB, INV, SP, SPR, SR, SD, SH, SX, SC = (
    0, 1, 2, 3, 4, 5, 6, 7, 8, 10, 14, 18, 22, 26,
)
N_SEM = 30


def main_kernel(
    ft, wt, labels, inv, order, block_starts, out,
    fa, wv, wn, wide, picks, iv, a, mem, fb, o, term_send, acc, p, m,
    got_p, r0, r_send, r_full, d_part, d_got, d_own, h_own, h_full, c_part, c_got, high, low,
    send, recv, load,
):
    y = lax.axis_index("sy")
    x = lax.axis_index("sx")
    c = lax.axis_index("sc")
    z = lax.axis_index("cols")
    chip = y * 4 + x
    shard = chip * 2 + c
    sib = (y, x, 1 - c, z)
    scale = 1.0 / math.sqrt(ROWS * 32)

    def peer(offset):
        row = lax.rem(y + offset // 4, 4)
        col = lax.rem(x + lax.rem(offset, 4), 4)
        return row, col, row * 4 + col

    loads = [
        pltpu.make_async_copy(ft, fa.at[pl.ds(0, WIDTH)], load.at[0]),
        pltpu.make_async_copy(wt, wv, load.at[1]),
        pltpu.make_async_copy(inv, iv.at[c], load.at[2]),
    ]
    for copy in loads:
        copy.start()

    barrier = pltpu.get_barrier_semaphore()

    def greet_plane(offset):
        row, col, _ = peer(offset)
        for core in range(2):

            @pl.when((offset > 0) | (core != c))
            def _():
                pl.semaphore_signal(
                    barrier, inc=1, device_id=(row, col, core, z), device_id_type=MESH
                )

    def greet_column(offset):
        for core in range(2):
            pl.semaphore_signal(
                barrier, inc=1, device_id=(y, x, core, lax.rem(z + offset, COLS)), device_id_type=MESH
            )

    over(0, CHIPS, greet_plane)
    over(1, COLS, greet_column)

    starts = []
    for t in range(UPD):
        start = jnp.int32(0)
        for block in range(BLOCKS):
            start += jnp.where(order[t] == block, block_starts[block], 0)
        starts.append(start)

    column = iota((1, LANES), 1)
    target = jnp.full((1, LANES), -1, jnp.int32)
    for t in range(UPD):
        here = column // PIECE == t
        target = jnp.where(here, starts[t] + z * PIECE + lax.rem(column, PIECE), target)
    picks[...] = (iota((ROWS, LANES), 0) == target).astype(BF16)
    loads[0].wait()
    chosen = dot(fa[0:WIDTH, :], picks[...])
    norm = jnp.sum(jnp.square(chosen), axis=0, keepdims=True)
    line = iota((8, LANES), 0)
    extra = jnp.where(line < 6, 1.0, 0.0)
    for number, part in enumerate(split3(norm)):
        extra = jnp.where(line == number + 3, -part, extra)
    rest = jnp.zeros((DEPTH - WIDTH - 8, LANES), F32)
    chosen = jnp.concatenate([2.0 * chosen, extra, rest], axis=0).T.astype(BF16)
    for t in range(UPD):
        mem[t] = chosen[t * PIECE : (t + 1) * PIECE]

    pl.semaphore_wait(barrier, 31 + 14)

    def send_members(first, count, number):
        def body(offset):
            row, col, _ = peer(offset)
            push(
                mem.at[pl.ds(first, count)],
                a.at[pl.ds(first, count), chip, c],
                send.at[number],
                recv.at[number],
                (row, col, c, z),
            )

        over(1, CHIPS, body)
        for t in range(first, first + count):
            a[t, chip, c] = mem[t]

    def forward_members(first, count, number, onward):
        drain(a.at[pl.ds(first, count), pl.ds(0, 15), 0], recv.at[number])
        ours = a.at[pl.ds(first, count), :, c]
        push(ours, ours, send.at[onward], recv.at[onward], sib)

    send_members(0, 1, MEM)
    send_members(1, 3, MEM_REST)

    line = iota((8, NBLOCK), 0)
    for block in range(ROWS // NBLOCK):
        cols = pl.ds(block * NBLOCK, NBLOCK)
        norm = jnp.sum(jnp.square(fa[0:WIDTH, cols].astype(F32)), axis=0, keepdims=True)
        extra = jnp.where(line < 6, 1.0, 0.0)
        for number, part in enumerate(split3(norm)):
            extra = jnp.where(line == number, -part, extra)
        tail = fa[432:440, cols].astype(F32)
        fa[432:448, cols] = jnp.concatenate([tail, extra], axis=0).astype(BF16)
        fa[448:DEPTH, cols] = jnp.zeros((DEPTH - 448, NBLOCK), BF16)

    loads[1].wait()
    values = [dot(part.astype(BF16), picks[...]) for part in split3(wv[...])]
    values = values[0] + values[1] + values[2]
    known = dot(jnp.broadcast_to(labels[...].astype(F32), (8, ROWS)).astype(BF16), picks[...])
    onehot = (iota((CLASSES, LANES), 0).astype(F32) == known[0:1]).astype(F32)
    wide[...] = jnp.zeros_like(wide)
    wide[0:CLASSES, :] = onehot - RIDGE * values
    terms = wide[...].T
    for t in range(UPD):
        first = terms[t * PIECE : (t + 1) * PIECE, 0:LANES]
        second = terms[t * PIECE : (t + 1) * PIECE, LANES:]
        o[t, c] = jnp.where(c == 0, first, second)
        term_send[t] = jnp.where(c == 0, second, first)
    push(term_send, o.at[:, c], send.at[TERM], recv.at[TERM], sib)
    for t in range(UPD - 1):
        picks[...] = (iota((ROWS, SPAN), 0) == starts[t] + iota((1, SPAN), 1)).astype(BF16)
        fb[c, t] = dot(fa[...], picks[...]).astype(BF16)
    push(fb.at[c], fb.at[c], send.at[FB], recv.at[FB], sib)
    push(inv, iv.at[c], send.at[INV], recv.at[INV], sib)
    for block in range(ROWS // NBLOCK):
        cols = pl.ds(block * NBLOCK, NBLOCK)
        wn[cols, :] = jnp.zeros((NBLOCK, 2 * LANES), BF16)
        wn[cols, 0:CLASSES] = wv[:, cols].T.astype(BF16)

    def panel(t, first, last):
        def body(block):
            cols = pl.ds(pl.multiple_of(block * NBLOCK, NBLOCK), NBLOCK)
            for half in range(2):
                rows = pl.ds(half * 256, 256)
                lines = a[t, pl.ds(half * 8, 8)].reshape(256, DEPTH)
                values = kernel_values(dot(lines, fa[:, cols]))
                acc[rows, :] += dot(values, wn[cols, :])

        if first == 0:
            acc[...] = jnp.zeros_like(acc)
        over(first, last, body)
        if last == ROWS // NBLOCK:
            for half in range(2):
                part = acc[:, half * LANES : (half + 1) * LANES].astype(BF16)
                p[half, t] = part.reshape(CHIPS, 32, LANES)

    def margin(early, late):
        lines = a[late].reshape(GROUP, DEPTH)
        for half in range(2):
            m[EARLIER.index((early, late)), half] = kernel_values(dot(lines, fb[half, early]))

    def send_products(first, count, number):
        def body(offset):
            row, col, other = peer(offset)
            for core in range(2):

                @pl.when((offset > 0) | (core != c))
                def _():
                    push(
                        p.at[core, pl.ds(first, count), other],
                        got_p.at[pl.ds(first, count), shard],
                        send.at[number],
                        recv.at[number],
                        (row, col, core, z),
                    )

        over(0, CHIPS, body)

    def sums_of_products(first, count, number):
        drain(got_p.at[pl.ds(first, count), pl.ds(0, 31)], recv.at[number])
        for t in range(first, first + count):
            got_p[t, shard] = p[c, t, chip]
            own = o[t].reshape(32, LANES)
            r0[t] = own - scale * jnp.sum(got_p[t].astype(F32), axis=0)

    def send_residual(t):
        def body(offset):
            row, col, _ = peer(offset)
            push(r_send.at[t], r_full.at[t, chip], send.at[SR + t], recv.at[SR + t], (row, col, c, z))

        over(1, CHIPS, body)
        r_full[t, chip] = r_send[t]

    def split_inverse(t):
        for half in range(2):
            value = iv[half, t]
            top = value.astype(BF16)
            high[t, half] = top
            low[t, half] = (value - top.astype(F32)).astype(BF16)

    def partial_delta(t):
        drain(r_full.at[t, pl.ds(0, 15)], recv.at[SR + t])
        residual = r_full[t].reshape(GROUP, LANES)
        top = residual.astype(BF16)
        rest = (residual - top.astype(F32)).astype(BF16)
        for half in range(2):
            value = dot(high[t, half], top) + dot(high[t, half], rest) + dot(low[t, half], top)
            d_part[t, pl.ds(half * 4, 4)] = value.reshape(4, 32, LANES)

        def body(offset):
            other = lax.rem(z + offset, COLS)
            push(d_part.at[t, other], d_got.at[t, z], send.at[SD + t], recv.at[SD + t], (y, x, c, other))

        over(1, COLS, body)
        d_got[t, z] = d_part[t, z]

    keeper = z // 4
    place = pl.ds(pl.multiple_of(lax.rem(z, 4) * 32, 32), 32)

    def finish_delta(t):
        drain(d_got.at[t, pl.ds(0, 7)], recv.at[SD + t])
        delta = jnp.sum(d_got[t], axis=0)
        d_own[t] = delta
        if t < UPD - 1:
            h_own[t] = delta.astype(BF16)

            def send_high(offset):
                other = lax.rem(z + offset, COLS)
                push(h_own.at[t], h_full.at[t, z], send.at[SH + t], recv.at[SH + t], (y, x, c, other))

            over(1, COLS, send_high)
            h_full[t, z] = h_own[t]

        def send_result(offset):
            other = lax.rem(z + offset, COLS)

            @pl.when((offset > 0) | (keeper != c))
            def _():
                push(
                    d_own.at[t], out.at[t, c, place], send.at[SX + t], recv.at[SX + t],
                    (y, x, keeper, other),
                )

        over(0, COLS, send_result)

        @pl.when(keeper == c)
        def _():
            out[t, c, place] = d_own[t]

    def corrections(early, late):
        total = None
        for half in range(2):
            lines = h_full[early, pl.ds(half * 4, 4)].reshape(SPAN, LANES)
            part = dot(m[EARLIER.index((early, late)), half], lines)
            total = part if total is None else total + part
        return total

    def next_residual(t, partial):
        late = t + 1
        drain(h_full.at[t, pl.ds(0, 7)], recv.at[SH + t])
        part = corrections(t, late)
        partial = part if partial is None else partial + part
        c_part[t] = partial.astype(BF16).reshape(CHIPS, 32, LANES)

        def body(offset):
            row, col, other = peer(offset)
            push(
                c_part.at[t, other], c_got.at[t, chip], send.at[SC + t], recv.at[SC + t], (row, col, c, z)
            )

        over(1, CHIPS, body)
        c_got[t, chip] = c_part[t, chip]
        line = iota((32, 2 * SPAN), 0)
        column = iota((32, 2 * SPAN), 1)
        member = starts[late] + z * PIECE + lax.rem(line, PIECE)
        same = line // PIECE == column // SPAN
        shared = jnp.zeros((32, LANES), F32)
        for early in range(late):
            hit = same & (member == starts[early] + lax.rem(column, SPAN))
            shared += dot(
                jnp.where(hit, RIDGE, 0.0).astype(BF16), h_full[early].reshape(2 * SPAN, LANES)
            )
        drain(c_got.at[t, pl.ds(0, 15)], recv.at[SC + t])
        r_send[late] = r0[late] - shared - scale * jnp.sum(c_got[t].astype(F32), axis=0)
        send_residual(late)

    whole = ROWS // NBLOCK
    forward_members(0, 1, MEM, SIB)
    loads[2].wait()
    drain(a.at[pl.ds(0, 1), :, 1 - c], recv.at[SIB])
    panel(0, 0, whole // 2)
    forward_members(1, 3, MEM_REST, SIB_REST)
    panel(0, whole // 2, whole)
    send_products(0, 1, SP)
    drain(fb.at[1 - c], recv.at[FB])
    drain(iv.at[1 - c], recv.at[INV])
    drain(o.at[:, 1 - c], recv.at[TERM])
    drain(a.at[pl.ds(1, 3), :, 1 - c], recv.at[SIB_REST])
    split_inverse(0)
    panel(1, 0, whole)
    sums_of_products(0, 1, SP)
    r_send[0] = r0[0]
    send_residual(0)
    panel(2, 0, whole)
    partial_delta(0)
    send_products(1, 2, SPR)
    panel(3, 0, whole)
    finish_delta(0)
    send_products(3, 1, SPR + 1)
    margin(0, 1)
    next_residual_ready = None
    sums_of_products(1, 2, SPR)
    next_residual(0, next_residual_ready)
    for pair in ((0, 2), (1, 2)):
        margin(*pair)
    split_inverse(1)
    partial_delta(1)
    for pair in ((0, 3), (1, 3)):
        margin(*pair)
    finish_delta(1)
    sums_of_products(3, 1, SPR + 1)
    next_residual(1, corrections(0, 2))
    split_inverse(2)
    margin(2, 3)
    partial_delta(2)
    partial = corrections(0, 3) + corrections(1, 3)
    finish_delta(2)
    split_inverse(3)
    next_residual(2, partial)
    partial_delta(3)
    finish_delta(3)

    for t in range(UPD):

        @pl.when(keeper == c)
        def _():
            drain(d_got.at[t, pl.ds(0, 7)], recv.at[SX + t])
            drain(d_got.at[t, pl.ds(0, 7)], send.at[SX + t])

        @pl.when(keeper != c)
        def _():
            drain(d_got.at[t], recv.at[SX + t])
            drain(d_got.at[t], send.at[SX + t])

        drain(r_full.at[t, pl.ds(0, 15)], send.at[SR + t])
        drain(d_got.at[t, pl.ds(0, 7)], send.at[SD + t])
        if t < UPD - 1:
            drain(h_full.at[t, pl.ds(0, 7)], send.at[SH + t])
            drain(c_got.at[t, pl.ds(0, 15)], send.at[SC + t])
    drain(got_p.at[pl.ds(0, 1), pl.ds(0, 31)], send.at[SP])
    drain(got_p.at[pl.ds(0, 2), pl.ds(0, 31)], send.at[SPR])
    drain(got_p.at[pl.ds(0, 1), pl.ds(0, 31)], send.at[SPR + 1])
    drain(a.at[pl.ds(0, 1), pl.ds(0, 15), 0], send.at[MEM])
    drain(a.at[pl.ds(1, 3), pl.ds(0, 15), 0], send.at[MEM_REST])
    drain(a.at[pl.ds(0, 1), :, 0], send.at[SIB])
    drain(a.at[pl.ds(1, 3), :, 0], send.at[SIB_REST])
    drain(fb.at[0], send.at[FB])
    drain(iv.at[0], send.at[INV])
    drain(term_send, send.at[TERM])


def deltas_of(ft, wt, labels, inv, order, starts):
    vmem = pltpu.VMEM
    return pl.pallas_call(
        main_kernel,
        out_shape=jax.ShapeDtypeStruct((UPD, 2, SPAN, LANES), F32),
        in_specs=[ANY, ANY, VMEM, ANY, SMEM, SMEM],
        out_specs=VMEM,
        scratch_shapes=[
            vmem((DEPTH, ROWS), BF16),
            vmem((CLASSES, ROWS), F32),
            vmem((ROWS, 2 * LANES), BF16),
            vmem((2 * LANES, LANES), F32),
            vmem((ROWS, LANES), BF16),
            vmem((2, UPD, SPAN, GROUP), F32),
            vmem((UPD, CHIPS, 2, PIECE, DEPTH), BF16),
            vmem((UPD, PIECE, DEPTH), BF16),
            vmem((2, UPD - 1, DEPTH, SPAN), BF16),
            vmem((UPD, 2, PIECE, LANES), F32),
            vmem((UPD, PIECE, LANES), F32),
            vmem((GROUP, 2 * LANES), F32),
            vmem((2, UPD, CHIPS, 32, LANES), BF16),
            vmem((len(EARLIER), 2, GROUP, SPAN), BF16),
            vmem((UPD, 2 * CHIPS, 32, LANES), BF16),
            vmem((UPD, 32, LANES), F32),
            vmem((UPD, 32, LANES), F32),
            vmem((UPD, CHIPS, 32, LANES), F32),
            vmem((UPD, COLS, 32, LANES), F32),
            vmem((UPD, COLS, 32, LANES), F32),
            vmem((UPD, 32, LANES), F32),
            vmem((UPD - 1, 32, LANES), BF16),
            vmem((UPD - 1, COLS, 32, LANES), BF16),
            vmem((UPD - 1, CHIPS, 32, LANES), BF16),
            vmem((UPD - 1, CHIPS, 32, LANES), BF16),
            vmem((UPD, 2, SPAN, GROUP), BF16),
            vmem((UPD, 2, SPAN, GROUP), BF16),
            pltpu.SemaphoreType.DMA((N_SEM,)),
            pltpu.SemaphoreType.DMA((N_SEM,)),
            pltpu.SemaphoreType.DMA((3,)),
        ],
        compiler_params=pltpu.CompilerParams(
            collective_id=0, has_side_effects=True, vmem_limit_bytes=48 << 20
        ),
        name="updates",
    )(ft, wt, labels, inv, order, starts)


def add_kernel(wt, deltas, order, block_starts, out):
    out[...] = wt[...]
    for t in range(UPD):
        base, shift = window_of(block_starts[order[t]])
        rows = jnp.concatenate([deltas[t, 0].T, deltas[t, 1].T], axis=0)[:CLASSES]
        wide = jnp.concatenate([rows, jnp.zeros((CLASSES, WINDOW - SPAN), F32)], axis=1)
        out[:, pl.ds(base, WINDOW)] += pltpu.roll(wide, shift, 1)


def add_deltas(wt, deltas, order, starts):
    return pl.pallas_call(
        add_kernel,
        out_shape=jax.ShapeDtypeStruct(wt.shape, wt.dtype),
        in_specs=[VMEM, VMEM, SMEM, SMEM],
        out_specs=VMEM,
        compiler_params=pltpu.CompilerParams(vmem_limit_bytes=16 << 20),
        name="add_deltas",
    )(wt, deltas, order, starts)


def local(features, labels, weights, block_order, block_starts, inverses):
    wt = weights.T
    deltas = deltas_of(
        features.T, wt, labels.reshape(1, ROWS), inverses, block_order, block_starts
    )
    return add_deltas(wt, deltas, block_order, block_starts).T


def solution(mesh):
    finer = Mesh(
        mesh.devices.reshape(4, 4, 2, mesh.shape["cols"]), ("sy", "sx", "sc", "cols")
    )
    in_specs = (P(SAMPLES, None), P(SAMPLES), P(SAMPLES, None), P(), P(), P(None, SAMPLES, "cols"))
    return jax.shard_map(
        local, mesh=finer, in_specs=in_specs, out_specs=P(SAMPLES, None), check_vma=False
    )
```

```python
import math

import jax
import jax.numpy as jnp
from jax import lax
from jax.experimental import pallas as pl
from jax.experimental.pallas import tpu as pltpu
from jax.sharding import Mesh
from jax.sharding import PartitionSpec as P

SAMPLES = ("sy", "sx", "sc")
MESH = pl.DeviceIdType.MESH
HIGHEST = lax.Precision.HIGHEST
RIDGE = 0.5
UPD = 4
BLOCKS = 32
CHIPS = 16
COLS = 8
SPAN = 128
PIECE = 16
GROUP = 512
WIDTH = 440
DEPTH = 512
LANES = 128
CLASSES = 147
ROWS = 4096
NBLOCK = 1024
WINDOW = 256
EARLIER = [(early, late) for late in range(UPD) for early in range(late)]
VMEM = pl.BlockSpec(memory_space=pltpu.VMEM)
SMEM = pl.BlockSpec(memory_space=pltpu.SMEM)
ANY = pl.BlockSpec(memory_space=pltpu.HBM)
F32, BF16 = jnp.float32, jnp.bfloat16
NT = (((1,), (1,)), ((), ()))


def push(src, dst, send, recv, device):
    pltpu.make_async_remote_copy(
        src_ref=src,
        dst_ref=dst,
        send_sem=send,
        recv_sem=recv,
        device_id=device,
        device_id_type=MESH,
    ).start()


def drain(ref, sem):
    pltpu.make_async_copy(ref, ref, sem).wait()


def over(low, high, body):
    def step(index, carry):
        body(index)
        return carry

    lax.fori_loop(low, high, step, 0)


def iota(shape, dim):
    return lax.broadcasted_iota(jnp.int32, shape, dim)


def dot(a, b):
    return jnp.dot(a, b, preferred_element_type=F32)


def split3(value):
    high = value.astype(BF16).astype(F32)
    rest = value - high
    middle = rest.astype(BF16).astype(F32)
    return high, middle, rest - middle


def kernel_values(exponent):
    return jnp.exp2(exponent * (math.log2(math.e) / WIDTH)).astype(BF16)


def window_of(start):
    base = jnp.minimum(start // LANES, (ROWS - WINDOW) // LANES) * LANES
    return pl.multiple_of(base, LANES), start - base


MEM, MEM_REST, SIB, SIB_REST, TERM, FB, INV, SP, SPR, SR, SD, SH, SX, SC = (
    0, 1, 2, 3, 4, 5, 6, 7, 8, 10, 14, 18, 22, 26,
)
N_SEM = 30


def main_kernel(
    ft, wt, labels, inv, order, block_starts, out,
    fa, wv, wn, wide, picks, iv, a, mem, fb, o, term_send, acc, p, m,
    got_p, r0, r_send, r_full, d_part, d_got, d_own, h_own, h_full, c_part, c_got, high, low,
    send, recv, load,
):
    y = lax.axis_index("sy")
    x = lax.axis_index("sx")
    c = lax.axis_index("sc")
    z = lax.axis_index("cols")
    chip = y * 4 + x
    shard = chip * 2 + c
    sib = (y, x, 1 - c, z)
    scale = 1.0 / math.sqrt(ROWS * 32)

    def peer(offset):
        row = lax.rem(y + offset // 4, 4)
        col = lax.rem(x + lax.rem(offset, 4), 4)
        return row, col, row * 4 + col

    loads = [
        pltpu.make_async_copy(ft, fa.at[pl.ds(0, WIDTH)], load.at[0]),
        pltpu.make_async_copy(wt, wv, load.at[1]),
        pltpu.make_async_copy(inv, iv.at[c], load.at[2]),
    ]
    for copy in loads:
        copy.start()

    barrier = pltpu.get_barrier_semaphore()

    def greet_plane(offset):
        row, col, _ = peer(offset)
        for core in range(2):

            @pl.when((offset > 0) | (core != c))
            def _():
                pl.semaphore_signal(
                    barrier, inc=1, device_id=(row, col, core, z), device_id_type=MESH
                )

    def greet_column(offset):
        for core in range(2):
            pl.semaphore_signal(
                barrier, inc=1, device_id=(y, x, core, lax.rem(z + offset, COLS)), device_id_type=MESH
            )

    over(0, CHIPS, greet_plane)
    over(1, COLS, greet_column)

    starts = []
    for t in range(UPD):
        start = jnp.int32(0)
        for block in range(BLOCKS):
            start += jnp.where(order[t] == block, block_starts[block], 0)
        starts.append(start)

    column = iota((1, LANES), 1)
    target = jnp.full((1, LANES), -1, jnp.int32)
    for t in range(UPD):
        here = column // PIECE == t
        target = jnp.where(here, starts[t] + z * PIECE + lax.rem(column, PIECE), target)
    picks[...] = (iota((ROWS, LANES), 0) == target).astype(BF16)
    loads[0].wait()
    chosen = dot(fa[0:WIDTH, :], picks[...])
    norm = jnp.sum(jnp.square(chosen), axis=0, keepdims=True)
    line = iota((8, LANES), 0)
    extra = jnp.where(line < 6, 1.0, 0.0)
    for number, part in enumerate(split3(norm)):
        extra = jnp.where(line == number + 3, -part, extra)
    rest = jnp.zeros((DEPTH - WIDTH - 8, LANES), F32)
    chosen = jnp.concatenate([2.0 * chosen, extra, rest], axis=0).T.astype(BF16)
    for t in range(UPD):
        mem[t] = chosen[t * PIECE : (t + 1) * PIECE]

    pl.semaphore_wait(barrier, 31 + 14)

    def send_members(first, count, number):
        def body(offset):
            row, col, _ = peer(offset)
            push(
                mem.at[pl.ds(first, count)],
                a.at[pl.ds(first, count), chip, c],
                send.at[number],
                recv.at[number],
                (row, col, c, z),
            )

        over(1, CHIPS, body)
        for t in range(first, first + count):
            a[t, chip, c] = mem[t]

    def forward_members(first, count, number, onward):
        drain(a.at[pl.ds(first, count), pl.ds(0, 15), 0], recv.at[number])
        ours = a.at[pl.ds(first, count), :, c]
        push(ours, ours, send.at[onward], recv.at[onward], sib)

    send_members(0, 1, MEM)
    send_members(1, 3, MEM_REST)

    line = iota((8, NBLOCK), 0)
    for block in range(ROWS // NBLOCK):
        cols = pl.ds(block * NBLOCK, NBLOCK)
        norm = jnp.sum(jnp.square(fa[0:WIDTH, cols].astype(F32)), axis=0, keepdims=True)
        extra = jnp.where(line < 6, 1.0, 0.0)
        for number, part in enumerate(split3(norm)):
            extra = jnp.where(line == number, -part, extra)
        tail = fa[432:440, cols].astype(F32)
        fa[432:448, cols] = jnp.concatenate([tail, extra], axis=0).astype(BF16)
        fa[448:DEPTH, cols] = jnp.zeros((DEPTH - 448, NBLOCK), BF16)

    loads[1].wait()
    values = [dot(part.astype(BF16), picks[...]) for part in split3(wv[...])]
    values = values[0] + values[1] + values[2]
    known = dot(jnp.broadcast_to(labels[...].astype(F32), (8, ROWS)).astype(BF16), picks[...])
    onehot = (iota((CLASSES, LANES), 0).astype(F32) == known[0:1]).astype(F32)
    wide[...] = jnp.zeros_like(wide)
    wide[0:CLASSES, :] = onehot - RIDGE * values
    terms = wide[...].T
    for t in range(UPD):
        first = terms[t * PIECE : (t + 1) * PIECE, 0:LANES]
        second = terms[t * PIECE : (t + 1) * PIECE, LANES:]
        o[t, c] = jnp.where(c == 0, first, second)
        term_send[t] = jnp.where(c == 0, second, first)
    push(term_send, o.at[:, c], send.at[TERM], recv.at[TERM], sib)
    for t in range(UPD - 1):
        picks[...] = (iota((ROWS, SPAN), 0) == starts[t] + iota((1, SPAN), 1)).astype(BF16)
        fb[c, t] = dot(fa[...], picks[...]).astype(BF16)
    push(fb.at[c], fb.at[c], send.at[FB], recv.at[FB], sib)
    push(inv, iv.at[c], send.at[INV], recv.at[INV], sib)
    for block in range(ROWS // NBLOCK):
        cols = pl.ds(block * NBLOCK, NBLOCK)
        wn[cols, :] = jnp.zeros((NBLOCK, 2 * LANES), BF16)
        wn[cols, 0:CLASSES] = wv[:, cols].T.astype(BF16)

    def panel(t, first, last):
        def body(block):
            cols = pl.ds(pl.multiple_of(block * NBLOCK, NBLOCK), NBLOCK)
            for half in range(2):
                rows = pl.ds(half * 256, 256)
                lines = a[t, pl.ds(half * 8, 8)].reshape(256, DEPTH)
                values = kernel_values(dot(lines, fa[:, cols]))
                acc[rows, :] += dot(values, wn[cols, :])

        if first == 0:
            acc[...] = jnp.zeros_like(acc)
        over(first, last, body)
        if last == ROWS // NBLOCK:
            for half in range(2):
                part = acc[:, half * LANES : (half + 1) * LANES].astype(BF16)
                p[half, t] = part.reshape(CHIPS, 32, LANES)

    def margin(early, late):
        lines = a[late].reshape(GROUP, DEPTH)
        for half in range(2):
            m[EARLIER.index((early, late)), half] = kernel_values(dot(lines, fb[half, early]))

    def send_products(first, count, number):
        def body(offset):
            row, col, other = peer(offset)
            for core in range(2):

                @pl.when((offset > 0) | (core != c))
                def _():
                    push(
                        p.at[core, pl.ds(first, count), other],
                        got_p.at[pl.ds(first, count), shard],
                        send.at[number],
                        recv.at[number],
                        (row, col, core, z),
                    )

        over(0, CHIPS, body)

    def sums_of_products(first, count, number):
        drain(got_p.at[pl.ds(first, count), pl.ds(0, 31)], recv.at[number])
        for t in range(first, first + count):
            got_p[t, shard] = p[c, t, chip]
            own = o[t].reshape(32, LANES)
            r0[t] = own - scale * jnp.sum(got_p[t].astype(F32), axis=0)

    def send_residual(t):
        def body(offset):
            row, col, _ = peer(offset)
            push(r_send.at[t], r_full.at[t, chip], send.at[SR + t], recv.at[SR + t], (row, col, c, z))

        over(1, CHIPS, body)
        r_full[t, chip] = r_send[t]

    def split_inverse(t):
        for half in range(2):
            value = iv[half, t]
            top = value.astype(BF16)
            high[t, half] = top
            low[t, half] = (value - top.astype(F32)).astype(BF16)

    def partial_delta(t):
        drain(r_full.at[t, pl.ds(0, 15)], recv.at[SR + t])
        residual = r_full[t].reshape(GROUP, LANES)
        top = residual.astype(BF16)
        rest = (residual - top.astype(F32)).astype(BF16)
        for half in range(2):
            value = dot(high[t, half], top) + dot(high[t, half], rest) + dot(low[t, half], top)
            d_part[t, pl.ds(half * 4, 4)] = value.reshape(4, 32, LANES)

        def body(offset):
            other = lax.rem(z + offset, COLS)
            push(d_part.at[t, other], d_got.at[t, z], send.at[SD + t], recv.at[SD + t], (y, x, c, other))

        over(1, COLS, body)
        d_got[t, z] = d_part[t, z]

    keeper = z // 4
    place = pl.ds(pl.multiple_of(lax.rem(z, 4) * 32, 32), 32)

    def finish_delta(t):
        drain(d_got.at[t, pl.ds(0, 7)], recv.at[SD + t])
        delta = jnp.sum(d_got[t], axis=0)
        d_own[t] = delta
        if t < UPD - 1:
            h_own[t] = delta.astype(BF16)

            def send_high(offset):
                other = lax.rem(z + offset, COLS)
                push(h_own.at[t], h_full.at[t, z], send.at[SH + t], recv.at[SH + t], (y, x, c, other))

            over(1, COLS, send_high)
            h_full[t, z] = h_own[t]

        def send_result(offset):
            other = lax.rem(z + offset, COLS)

            @pl.when((offset > 0) | (keeper != c))
            def _():
                push(
                    d_own.at[t], out.at[t, c, place], send.at[SX + t], recv.at[SX + t],
                    (y, x, keeper, other),
                )

        over(0, COLS, send_result)

        @pl.when(keeper == c)
        def _():
            out[t, c, place] = d_own[t]

    def corrections(early, late):
        total = None
        for half in range(2):
            lines = h_full[early, pl.ds(half * 4, 4)].reshape(SPAN, LANES)
            part = dot(m[EARLIER.index((early, late)), half], lines)
            total = part if total is None else total + part
        return total

    def send_correction(t, partial):
        late = t + 1
        drain(h_full.at[t, pl.ds(0, 7)], recv.at[SH + t])
        part = corrections(t, late)
        partial = part if partial is None else partial + part
        c_part[t] = partial.astype(BF16).reshape(CHIPS, 32, LANES)

        def body(offset):
            row, col, other = peer(offset)
            push(
                c_part.at[t, other], c_got.at[t, chip], send.at[SC + t], recv.at[SC + t], (row, col, c, z)
            )

        over(1, CHIPS, body)
        c_got[t, chip] = c_part[t, chip]

    def next_residual(t):
        late = t + 1
        line = iota((32, 2 * SPAN), 0)
        column = iota((32, 2 * SPAN), 1)
        member = starts[late] + z * PIECE + lax.rem(line, PIECE)
        same = line // PIECE == column // SPAN
        shared = jnp.zeros((32, LANES), F32)
        for early in range(late):
            hit = same & (member == starts[early] + lax.rem(column, SPAN))
            shared += dot(
                jnp.where(hit, RIDGE, 0.0).astype(BF16), h_full[early].reshape(2 * SPAN, LANES)
            )
        drain(c_got.at[t, pl.ds(0, 15)], recv.at[SC + t])
        r_send[late] = r0[late] - shared - scale * jnp.sum(c_got[t].astype(F32), axis=0)
        send_residual(late)

    whole = ROWS // NBLOCK
    forward_members(0, 1, MEM, SIB)
    loads[2].wait()
    drain(a.at[pl.ds(0, 1), :, 1 - c], recv.at[SIB])
    panel(0, 0, whole // 2)
    forward_members(1, 3, MEM_REST, SIB_REST)
    panel(0, whole // 2, whole)
    send_products(0, 1, SP)
    drain(fb.at[1 - c], recv.at[FB])
    drain(iv.at[1 - c], recv.at[INV])
    drain(o.at[:, 1 - c], recv.at[TERM])
    drain(a.at[pl.ds(1, 3), :, 1 - c], recv.at[SIB_REST])
    split_inverse(0)
    panel(1, 0, whole)
    sums_of_products(0, 1, SP)
    r_send[0] = r0[0]
    send_residual(0)
    panel(2, 0, whole)
    partial_delta(0)
    send_products(1, 2, SPR)
    panel(3, 0, whole)
    finish_delta(0)
    send_products(3, 1, SPR + 1)
    margin(0, 1)
    send_correction(0, None)
    sums_of_products(1, 2, SPR)
    next_residual(0)
    split_inverse(1)
    partial_delta(1)
    margin(0, 2)
    margin(0, 3)
    partial = corrections(0, 2)
    finish_delta(1)
    margin(1, 2)
    margin(1, 3)
    send_correction(1, partial)
    sums_of_products(3, 1, SPR + 1)
    next_residual(1)
    split_inverse(2)
    partial_delta(2)
    partial = corrections(0, 3) + corrections(1, 3)
    finish_delta(2)
    margin(2, 3)
    send_correction(2, partial)
    split_inverse(3)
    next_residual(2)
    partial_delta(3)
    finish_delta(3)

    for t in range(UPD):

        @pl.when(keeper == c)
        def _():
            drain(d_got.at[t, pl.ds(0, 7)], recv.at[SX + t])
            drain(d_got.at[t, pl.ds(0, 7)], send.at[SX + t])

        @pl.when(keeper != c)
        def _():
            drain(d_got.at[t], recv.at[SX + t])
            drain(d_got.at[t], send.at[SX + t])

        drain(r_full.at[t, pl.ds(0, 15)], send.at[SR + t])
        drain(d_got.at[t, pl.ds(0, 7)], send.at[SD + t])
        if t < UPD - 1:
            drain(h_full.at[t, pl.ds(0, 7)], send.at[SH + t])
            drain(c_got.at[t, pl.ds(0, 15)], send.at[SC + t])
    drain(got_p.at[pl.ds(0, 1), pl.ds(0, 31)], send.at[SP])
    drain(got_p.at[pl.ds(0, 2), pl.ds(0, 31)], send.at[SPR])
    drain(got_p.at[pl.ds(0, 1), pl.ds(0, 31)], send.at[SPR + 1])
    drain(a.at[pl.ds(0, 1), pl.ds(0, 15), 0], send.at[MEM])
    drain(a.at[pl.ds(1, 3), pl.ds(0, 15), 0], send.at[MEM_REST])
    drain(a.at[pl.ds(0, 1), :, 0], send.at[SIB])
    drain(a.at[pl.ds(1, 3), :, 0], send.at[SIB_REST])
    drain(fb.at[0], send.at[FB])
    drain(iv.at[0], send.at[INV])
    drain(term_send, send.at[TERM])


def deltas_of(ft, wt, labels, inv, order, starts):
    vmem = pltpu.VMEM
    return pl.pallas_call(
        main_kernel,
        out_shape=jax.ShapeDtypeStruct((UPD, 2, SPAN, LANES), F32),
        in_specs=[ANY, ANY, VMEM, ANY, SMEM, SMEM],
        out_specs=VMEM,
        scratch_shapes=[
            vmem((DEPTH, ROWS), BF16),
            vmem((CLASSES, ROWS), F32),
            vmem((ROWS, 2 * LANES), BF16),
            vmem((2 * LANES, LANES), F32),
            vmem((ROWS, LANES), BF16),
            vmem((2, UPD, SPAN, GROUP), F32),
            vmem((UPD, CHIPS, 2, PIECE, DEPTH), BF16),
            vmem((UPD, PIECE, DEPTH), BF16),
            vmem((2, UPD - 1, DEPTH, SPAN), BF16),
            vmem((UPD, 2, PIECE, LANES), F32),
            vmem((UPD, PIECE, LANES), F32),
            vmem((GROUP, 2 * LANES), F32),
            vmem((2, UPD, CHIPS, 32, LANES), BF16),
            vmem((len(EARLIER), 2, GROUP, SPAN), BF16),
            vmem((UPD, 2 * CHIPS, 32, LANES), BF16),
            vmem((UPD, 32, LANES), F32),
            vmem((UPD, 32, LANES), F32),
            vmem((UPD, CHIPS, 32, LANES), F32),
            vmem((UPD, COLS, 32, LANES), F32),
            vmem((UPD, COLS, 32, LANES), F32),
            vmem((UPD, 32, LANES), F32),
            vmem((UPD - 1, 32, LANES), BF16),
            vmem((UPD - 1, COLS, 32, LANES), BF16),
            vmem((UPD - 1, CHIPS, 32, LANES), BF16),
            vmem((UPD - 1, CHIPS, 32, LANES), BF16),
            vmem((UPD, 2, SPAN, GROUP), BF16),
            vmem((UPD, 2, SPAN, GROUP), BF16),
            pltpu.SemaphoreType.DMA((N_SEM,)),
            pltpu.SemaphoreType.DMA((N_SEM,)),
            pltpu.SemaphoreType.DMA((3,)),
        ],
        compiler_params=pltpu.CompilerParams(
            collective_id=0, has_side_effects=True, vmem_limit_bytes=64 << 20
        ),
        name="updates",
    )(ft, wt, labels, inv, order, starts)


def add_kernel(wt, deltas, order, block_starts, out):
    out[...] = wt[...]
    for t in range(UPD):
        base, shift = window_of(block_starts[order[t]])
        rows = jnp.concatenate([deltas[t, 0].T, deltas[t, 1].T], axis=0)[:CLASSES]
        wide = jnp.concatenate([rows, jnp.zeros((CLASSES, WINDOW - SPAN), F32)], axis=1)
        out[:, pl.ds(base, WINDOW)] += pltpu.roll(wide, shift, 1)


def add_deltas(wt, deltas, order, starts):
    return pl.pallas_call(
        add_kernel,
        out_shape=jax.ShapeDtypeStruct(wt.shape, wt.dtype),
        in_specs=[VMEM, VMEM, SMEM, SMEM],
        out_specs=VMEM,
        compiler_params=pltpu.CompilerParams(vmem_limit_bytes=64 << 20),
        name="add_deltas",
    )(wt, deltas, order, starts)


def local(features, labels, weights, block_order, block_starts, inverses):
    wt = weights.T
    deltas = deltas_of(
        features.T, wt, labels.reshape(1, ROWS), inverses, block_order, block_starts
    )
    return add_deltas(wt, deltas, block_order, block_starts).T


def solution(mesh):
    finer = Mesh(
        mesh.devices.reshape(4, 4, 2, mesh.shape["cols"]), ("sy", "sx", "sc", "cols")
    )
    in_specs = (P(SAMPLES, None), P(SAMPLES), P(SAMPLES, None), P(), P(), P(None, SAMPLES, "cols"))
    return jax.shard_map(
        local, mesh=finer, in_specs=in_specs, out_specs=P(SAMPLES, None), check_vma=False
    )
```

```python
import math

import jax
import jax.numpy as jnp
from jax import lax
from jax.experimental import pallas as pl
from jax.experimental.pallas import tpu as pltpu
from jax.sharding import Mesh
from jax.sharding import PartitionSpec as P

SAMPLES = ("sy", "sx", "sc")
MESH = pl.DeviceIdType.MESH
HIGHEST = lax.Precision.HIGHEST
RIDGE = 0.5
UPD = 4
BLOCKS = 32
CHIPS = 16
COLS = 8
SPAN = 128
PIECE = 16
GROUP = 512
WIDTH = 440
DEPTH = 512
LANES = 128
CLASSES = 147
ROWS = 4096
NBLOCK = 1024
WINDOW = 256
EARLIER = [(early, late) for late in range(UPD) for early in range(late)]
VMEM = pl.BlockSpec(memory_space=pltpu.VMEM)
SMEM = pl.BlockSpec(memory_space=pltpu.SMEM)
ANY = pl.BlockSpec(memory_space=pltpu.HBM)
F32, BF16 = jnp.float32, jnp.bfloat16
NT = (((1,), (1,)), ((), ()))


def push(src, dst, send, recv, device):
    pltpu.make_async_remote_copy(
        src_ref=src,
        dst_ref=dst,
        send_sem=send,
        recv_sem=recv,
        device_id=device,
        device_id_type=MESH,
    ).start()


def drain(ref, sem):
    pltpu.make_async_copy(ref, ref, sem).wait()


def over(low, high, body):
    def step(index, carry):
        body(index)
        return carry

    lax.fori_loop(low, high, step, 0)


def iota(shape, dim):
    return lax.broadcasted_iota(jnp.int32, shape, dim)


def dot(a, b):
    return jnp.dot(a, b, preferred_element_type=F32)


def split3(value):
    high = value.astype(BF16).astype(F32)
    rest = value - high
    middle = rest.astype(BF16).astype(F32)
    return high, middle, rest - middle


def kernel_values(exponent):
    return jnp.exp2(exponent * (math.log2(math.e) / WIDTH)).astype(BF16)


def window_of(start):
    base = jnp.minimum(start // LANES, (ROWS - WINDOW) // LANES) * LANES
    return pl.multiple_of(base, LANES), start - base


MEM, MEM_REST, SIB, SIB_REST, TERM, FB, INV, SP, SPR, SR, SD, SH, SX, SC = (
    0, 1, 2, 3, 4, 5, 6, 7, 8, 10, 14, 18, 22, 26,
)
N_SEM = 30


def main_kernel(
    ft, wt, labels, inv, order, block_starts, out,
    fa, wv, wn, wide, picks, iv, a, mem, fb, o, term_send, acc, p, m,
    got_p, r0, r_send, r_full, d_part, d_got, d_own, h_own, h_full, c_part, c_got, high, low,
    send, recv, load,
):
    y = lax.axis_index("sy")
    x = lax.axis_index("sx")
    c = lax.axis_index("sc")
    z = lax.axis_index("cols")
    chip = y * 4 + x
    shard = chip * 2 + c
    sib = (y, x, 1 - c, z)
    scale = 1.0 / math.sqrt(ROWS * 32)

    def peer(offset):
        row = lax.rem(y + offset // 4, 4)
        col = lax.rem(x + lax.rem(offset, 4), 4)
        return row, col, row * 4 + col

    loads = [
        pltpu.make_async_copy(ft, fa.at[pl.ds(0, WIDTH)], load.at[0]),
        pltpu.make_async_copy(wt, wv, load.at[1]),
        pltpu.make_async_copy(inv, iv.at[c], load.at[2]),
    ]
    for copy in loads:
        copy.start()

    barrier = pltpu.get_barrier_semaphore()

    def greet_plane(offset):
        row, col, _ = peer(offset)
        for core in range(2):

            @pl.when((offset > 0) | (core != c))
            def _():
                pl.semaphore_signal(
                    barrier, inc=1, device_id=(row, col, core, z), device_id_type=MESH
                )

    def greet_column(offset):
        for core in range(2):
            pl.semaphore_signal(
                barrier, inc=1, device_id=(y, x, core, lax.rem(z + offset, COLS)), device_id_type=MESH
            )

    over(0, CHIPS, greet_plane)
    over(1, COLS, greet_column)

    starts = []
    for t in range(UPD):
        start = jnp.int32(0)
        for block in range(BLOCKS):
            start += jnp.where(order[t] == block, block_starts[block], 0)
        starts.append(start)

    column = iota((1, LANES), 1)
    target = jnp.full((1, LANES), -1, jnp.int32)
    for t in range(UPD):
        here = column // PIECE == t
        target = jnp.where(here, starts[t] + z * PIECE + lax.rem(column, PIECE), target)
    picks[...] = (iota((ROWS, LANES), 0) == target).astype(BF16)
    loads[0].wait()
    chosen = dot(fa[0:WIDTH, :], picks[...])
    norm = jnp.sum(jnp.square(chosen), axis=0, keepdims=True)
    line = iota((8, LANES), 0)
    extra = jnp.where(line < 6, 1.0, 0.0)
    for number, part in enumerate(split3(norm)):
        extra = jnp.where(line == number + 3, -part, extra)
    rest = jnp.zeros((DEPTH - WIDTH - 8, LANES), F32)
    chosen = jnp.concatenate([2.0 * chosen, extra, rest], axis=0).T.astype(BF16)
    for t in range(UPD):
        mem[t] = chosen[t * PIECE : (t + 1) * PIECE]

    pl.semaphore_wait(barrier, 31 + 14)

    def send_members(first, count, number):
        def body(offset):
            row, col, _ = peer(offset)
            push(
                mem.at[pl.ds(first, count)],
                a.at[pl.ds(first, count), chip, c],
                send.at[number],
                recv.at[number],
                (row, col, c, z),
            )

        over(1, CHIPS, body)
        for t in range(first, first + count):
            a[t, chip, c] = mem[t]

    def forward_members(first, count, number, onward):
        drain(a.at[pl.ds(first, count), pl.ds(0, 15), 0], recv.at[number])
        ours = a.at[pl.ds(first, count), :, c]
        push(ours, ours, send.at[onward], recv.at[onward], sib)

    send_members(0, 1, MEM)
    send_members(1, 3, MEM_REST)

    line = iota((8, NBLOCK), 0)
    for block in range(ROWS // NBLOCK):
        cols = pl.ds(block * NBLOCK, NBLOCK)
        norm = jnp.sum(jnp.square(fa[0:WIDTH, cols].astype(F32)), axis=0, keepdims=True)
        extra = jnp.where(line < 6, 1.0, 0.0)
        for number, part in enumerate(split3(norm)):
            extra = jnp.where(line == number, -part, extra)
        tail = fa[432:440, cols].astype(F32)
        fa[432:448, cols] = jnp.concatenate([tail, extra], axis=0).astype(BF16)
        fa[448:DEPTH, cols] = jnp.zeros((DEPTH - 448, NBLOCK), BF16)

    loads[1].wait()
    values = [dot(part.astype(BF16), picks[...]) for part in split3(wv[...])]
    values = values[0] + values[1] + values[2]
    known = dot(jnp.broadcast_to(labels[...].astype(F32), (8, ROWS)).astype(BF16), picks[...])
    onehot = (iota((CLASSES, LANES), 0).astype(F32) == known[0:1]).astype(F32)
    wide[...] = jnp.zeros_like(wide)
    wide[0:CLASSES, :] = onehot - RIDGE * values
    terms = wide[...].T
    for t in range(UPD):
        first = terms[t * PIECE : (t + 1) * PIECE, 0:LANES]
        second = terms[t * PIECE : (t + 1) * PIECE, LANES:]
        o[t, c] = jnp.where(c == 0, first, second)
        term_send[t] = jnp.where(c == 0, second, first)
    push(term_send, o.at[:, c], send.at[TERM], recv.at[TERM], sib)
    for t in range(UPD - 1):
        picks[...] = (iota((ROWS, SPAN), 0) == starts[t] + iota((1, SPAN), 1)).astype(BF16)
        fb[c, t] = dot(fa[...], picks[...]).astype(BF16)
    push(fb.at[c], fb.at[c], send.at[FB], recv.at[FB], sib)
    push(inv, iv.at[c], send.at[INV], recv.at[INV], sib)
    for block in range(ROWS // NBLOCK):
        cols = pl.ds(block * NBLOCK, NBLOCK)
        wn[cols, :] = jnp.zeros((NBLOCK, 2 * LANES), BF16)
        wn[cols, 0:CLASSES] = wv[:, cols].T.astype(BF16)

    def panel(t, first, last):
        def body(block):
            cols = pl.ds(pl.multiple_of(block * NBLOCK, NBLOCK), NBLOCK)
            for half in range(2):
                rows = pl.ds(half * 256, 256)
                lines = a[t, pl.ds(half * 8, 8)].reshape(256, DEPTH)
                values = kernel_values(dot(lines, fa[:, cols]))
                acc[rows, :] += dot(values, wn[cols, :])

        if first == 0:
            acc[...] = jnp.zeros_like(acc)
        over(first, last, body)
        if last == ROWS // NBLOCK:
            for half in range(2):
                part = acc[:, half * LANES : (half + 1) * LANES].astype(BF16)
                p[half, t] = part.reshape(CHIPS, 32, LANES)

    def margin(early, late):
        lines = a[late].reshape(GROUP, DEPTH)
        for half in range(2):
            m[EARLIER.index((early, late)), half] = kernel_values(dot(lines, fb[half, early]))

    def send_products(first, count, number):
        def body(offset):
            row, col, other = peer(offset)
            for core in range(2):

                @pl.when((offset > 0) | (core != c))
                def _():
                    push(
                        p.at[core, pl.ds(first, count), other],
                        got_p.at[pl.ds(first, count), shard],
                        send.at[number],
                        recv.at[number],
                        (row, col, core, z),
                    )

        over(0, CHIPS, body)

    def sums_of_products(first, count, number):
        drain(got_p.at[pl.ds(first, count), pl.ds(0, 31)], recv.at[number])
        for t in range(first, first + count):
            got_p[t, shard] = p[c, t, chip]
            own = o[t].reshape(32, LANES)
            r0[t] = own - scale * jnp.sum(got_p[t].astype(F32), axis=0)

    def send_residual(t):
        def body(offset):
            row, col, _ = peer(offset)
            push(r_send.at[t], r_full.at[t, chip], send.at[SR + t], recv.at[SR + t], (row, col, c, z))

        over(1, CHIPS, body)
        r_full[t, chip] = r_send[t]

    def split_inverse(t):
        for half in range(2):
            value = iv[half, t]
            top = value.astype(BF16)
            high[t, half] = top
            low[t, half] = (value - top.astype(F32)).astype(BF16)

    def partial_delta(t):
        drain(r_full.at[t, pl.ds(0, 15)], recv.at[SR + t])
        residual = r_full[t].reshape(GROUP, LANES)
        top = residual.astype(BF16)
        rest = (residual - top.astype(F32)).astype(BF16)
        for half in range(2):
            value = dot(high[t, half], top) + dot(high[t, half], rest) + dot(low[t, half], top)
            d_part[t, pl.ds(half * 4, 4)] = value.reshape(4, 32, LANES)

        def body(offset):
            other = lax.rem(z + offset, COLS)
            push(d_part.at[t, other], d_got.at[t, z], send.at[SD + t], recv.at[SD + t], (y, x, c, other))

        over(1, COLS, body)
        d_got[t, z] = d_part[t, z]

    keeper = z // 4
    place = pl.ds(pl.multiple_of(lax.rem(z, 4) * 32, 32), 32)

    def finish_delta(t):
        drain(d_got.at[t, pl.ds(0, 7)], recv.at[SD + t])
        delta = jnp.sum(d_got[t], axis=0)
        d_own[t] = delta
        if t < UPD - 1:
            h_own[t] = delta.astype(BF16)

            def send_high(offset):
                other = lax.rem(z + offset, COLS)
                push(h_own.at[t], h_full.at[t, z], send.at[SH + t], recv.at[SH + t], (y, x, c, other))

            over(1, COLS, send_high)
            h_full[t, z] = h_own[t]

        def send_result(offset):
            other = lax.rem(z + offset, COLS)

            @pl.when((offset > 0) | (keeper != c))
            def _():
                push(
                    d_own.at[t], out.at[t, c, place], send.at[SX + t], recv.at[SX + t],
                    (y, x, keeper, other),
                )

        over(0, COLS, send_result)

        @pl.when(keeper == c)
        def _():
            out[t, c, place] = d_own[t]

    def corrections(early, late):
        total = None
        for half in range(2):
            lines = h_full[early, pl.ds(half * 4, 4)].reshape(SPAN, LANES)
            part = dot(m[EARLIER.index((early, late)), half], lines)
            total = part if total is None else total + part
        return total

    def send_correction(t, partial):
        late = t + 1
        drain(h_full.at[t, pl.ds(0, 7)], recv.at[SH + t])
        part = corrections(t, late)
        partial = part if partial is None else partial + part
        c_part[t] = partial.astype(BF16).reshape(CHIPS, 32, LANES)

        def body(offset):
            row, col, other = peer(offset)
            push(
                c_part.at[t, other], c_got.at[t, chip], send.at[SC + t], recv.at[SC + t], (row, col, c, z)
            )

        over(1, CHIPS, body)
        c_got[t, chip] = c_part[t, chip]

    def next_residual(t):
        late = t + 1
        line = iota((32, 2 * SPAN), 0)
        column = iota((32, 2 * SPAN), 1)
        member = starts[late] + z * PIECE + lax.rem(line, PIECE)
        same = line // PIECE == column // SPAN
        shared = jnp.zeros((32, LANES), F32)
        for early in range(late):
            hit = same & (member == starts[early] + lax.rem(column, SPAN))
            shared += dot(
                jnp.where(hit, RIDGE, 0.0).astype(BF16), h_full[early].reshape(2 * SPAN, LANES)
            )
        drain(c_got.at[t, pl.ds(0, 15)], recv.at[SC + t])
        r_send[late] = r0[late] - shared - scale * jnp.sum(c_got[t].astype(F32), axis=0)
        send_residual(late)

    whole = ROWS // NBLOCK
    forward_members(0, 1, MEM, SIB)
    loads[2].wait()
    drain(a.at[pl.ds(0, 1), :, 1 - c], recv.at[SIB])
    panel(0, 0, whole)
    send_products(0, 1, SP)
    forward_members(1, 3, MEM_REST, SIB_REST)
    drain(iv.at[1 - c], recv.at[INV])
    split_inverse(1)
    drain(fb.at[1 - c], recv.at[FB])
    drain(o.at[:, 1 - c], recv.at[TERM])
    drain(a.at[pl.ds(1, 3), :, 1 - c], recv.at[SIB_REST])
    split_inverse(0)
    panel(1, 0, whole)
    sums_of_products(0, 1, SP)
    r_send[0] = r0[0]
    send_residual(0)
    panel(2, 0, whole)
    partial_delta(0)
    send_products(1, 2, SPR)
    panel(3, 0, whole)
    finish_delta(0)
    send_products(3, 1, SPR + 1)
    margin(0, 1)
    send_correction(0, None)
    sums_of_products(1, 2, SPR)
    next_residual(0)
    partial_delta(1)
    margin(0, 2)
    margin(0, 3)
    partial = corrections(0, 2)
    finish_delta(1)
    margin(1, 2)
    margin(1, 3)
    send_correction(1, partial)
    sums_of_products(3, 1, SPR + 1)
    next_residual(1)
    split_inverse(2)
    partial_delta(2)
    partial = corrections(0, 3) + corrections(1, 3)
    finish_delta(2)
    margin(2, 3)
    send_correction(2, partial)
    split_inverse(3)
    next_residual(2)
    partial_delta(3)
    finish_delta(3)

    for t in range(UPD):

        @pl.when(keeper == c)
        def _():
            drain(d_got.at[t, pl.ds(0, 7)], recv.at[SX + t])
            drain(d_got.at[t, pl.ds(0, 7)], send.at[SX + t])

        @pl.when(keeper != c)
        def _():
            drain(d_got.at[t], recv.at[SX + t])
            drain(d_got.at[t], send.at[SX + t])

        drain(r_full.at[t, pl.ds(0, 15)], send.at[SR + t])
        drain(d_got.at[t, pl.ds(0, 7)], send.at[SD + t])
        if t < UPD - 1:
            drain(h_full.at[t, pl.ds(0, 7)], send.at[SH + t])
            drain(c_got.at[t, pl.ds(0, 15)], send.at[SC + t])
    drain(got_p.at[pl.ds(0, 1), pl.ds(0, 31)], send.at[SP])
    drain(got_p.at[pl.ds(0, 2), pl.ds(0, 31)], send.at[SPR])
    drain(got_p.at[pl.ds(0, 1), pl.ds(0, 31)], send.at[SPR + 1])
    drain(a.at[pl.ds(0, 1), pl.ds(0, 15), 0], send.at[MEM])
    drain(a.at[pl.ds(1, 3), pl.ds(0, 15), 0], send.at[MEM_REST])
    drain(a.at[pl.ds(0, 1), :, 0], send.at[SIB])
    drain(a.at[pl.ds(1, 3), :, 0], send.at[SIB_REST])
    drain(fb.at[0], send.at[FB])
    drain(iv.at[0], send.at[INV])
    drain(term_send, send.at[TERM])


def deltas_of(ft, wt, labels, inv, order, starts):
    vmem = pltpu.VMEM
    return pl.pallas_call(
        main_kernel,
        out_shape=jax.ShapeDtypeStruct((UPD, 2, SPAN, LANES), F32),
        in_specs=[ANY, ANY, VMEM, ANY, SMEM, SMEM],
        out_specs=VMEM,
        scratch_shapes=[
            vmem((DEPTH, ROWS), BF16),
            vmem((CLASSES, ROWS), F32),
            vmem((ROWS, 2 * LANES), BF16),
            vmem((2 * LANES, LANES), F32),
            vmem((ROWS, LANES), BF16),
            vmem((2, UPD, SPAN, GROUP), F32),
            vmem((UPD, CHIPS, 2, PIECE, DEPTH), BF16),
            vmem((UPD, PIECE, DEPTH), BF16),
            vmem((2, UPD - 1, DEPTH, SPAN), BF16),
            vmem((UPD, 2, PIECE, LANES), F32),
            vmem((UPD, PIECE, LANES), F32),
            vmem((GROUP, 2 * LANES), F32),
            vmem((2, UPD, CHIPS, 32, LANES), BF16),
            vmem((len(EARLIER), 2, GROUP, SPAN), BF16),
            vmem((UPD, 2 * CHIPS, 32, LANES), BF16),
            vmem((UPD, 32, LANES), F32),
            vmem((UPD, 32, LANES), F32),
            vmem((UPD, CHIPS, 32, LANES), F32),
            vmem((UPD, COLS, 32, LANES), F32),
            vmem((UPD, COLS, 32, LANES), F32),
            vmem((UPD, 32, LANES), F32),
            vmem((UPD - 1, 32, LANES), BF16),
            vmem((UPD - 1, COLS, 32, LANES), BF16),
            vmem((UPD - 1, CHIPS, 32, LANES), BF16),
            vmem((UPD - 1, CHIPS, 32, LANES), BF16),
            vmem((UPD, 2, SPAN, GROUP), BF16),
            vmem((UPD, 2, SPAN, GROUP), BF16),
            pltpu.SemaphoreType.DMA((N_SEM,)),
            pltpu.SemaphoreType.DMA((N_SEM,)),
            pltpu.SemaphoreType.DMA((3,)),
        ],
        compiler_params=pltpu.CompilerParams(
            collective_id=0, has_side_effects=True, vmem_limit_bytes=64 << 20
        ),
        name="updates",
    )(ft, wt, labels, inv, order, starts)


def add_kernel(wt, deltas, order, block_starts, out):
    out[...] = wt[...]
    for t in range(UPD):
        base, shift = window_of(block_starts[order[t]])
        rows = jnp.concatenate([deltas[t, 0].T, deltas[t, 1].T], axis=0)[:CLASSES]
        wide = jnp.concatenate([rows, jnp.zeros((CLASSES, WINDOW - SPAN), F32)], axis=1)
        out[:, pl.ds(base, WINDOW)] += pltpu.roll(wide, shift, 1)


def add_deltas(wt, deltas, order, starts):
    return pl.pallas_call(
        add_kernel,
        out_shape=jax.ShapeDtypeStruct(wt.shape, wt.dtype),
        in_specs=[VMEM, VMEM, SMEM, SMEM],
        out_specs=VMEM,
        compiler_params=pltpu.CompilerParams(vmem_limit_bytes=64 << 20),
        name="add_deltas",
    )(wt, deltas, order, starts)


def local(features, labels, weights, block_order, block_starts, inverses):
    wt = weights.T
    deltas = deltas_of(
        features.T, wt, labels.reshape(1, ROWS), inverses, block_order, block_starts
    )
    return add_deltas(wt, deltas, block_order, block_starts).T


def solution(mesh):
    finer = Mesh(
        mesh.devices.reshape(4, 4, 2, mesh.shape["cols"]), ("sy", "sx", "sc", "cols")
    )
    in_specs = (P(SAMPLES, None), P(SAMPLES), P(SAMPLES, None), P(), P(), P(None, SAMPLES, "cols"))
    return jax.shard_map(
        local, mesh=finer, in_specs=in_specs, out_specs=P(SAMPLES, None), check_vma=False
    )
```

```python
import math

import jax
import jax.numpy as jnp
from jax import lax
from jax.experimental import pallas as pl
from jax.experimental.pallas import tpu as pltpu
from jax.sharding import Mesh
from jax.sharding import PartitionSpec as P

SAMPLES = ("sy", "sx", "sc")
MESH = pl.DeviceIdType.MESH
HIGHEST = lax.Precision.HIGHEST
RIDGE = 0.5
UPD = 4
BLOCKS = 32
CHIPS = 16
COLS = 8
SPAN = 128
PIECE = 16
GROUP = 512
WIDTH = 440
DEPTH = 512
LANES = 128
CLASSES = 147
ROWS = 4096
NBLOCK = 1024
WINDOW = 256
EARLIER = [(early, late) for late in range(UPD) for early in range(late)]
VMEM = pl.BlockSpec(memory_space=pltpu.VMEM)
SMEM = pl.BlockSpec(memory_space=pltpu.SMEM)
ANY = pl.BlockSpec(memory_space=pltpu.HBM)
F32, BF16 = jnp.float32, jnp.bfloat16
NT = (((1,), (1,)), ((), ()))


def push(src, dst, send, recv, device):
    pltpu.make_async_remote_copy(
        src_ref=src,
        dst_ref=dst,
        send_sem=send,
        recv_sem=recv,
        device_id=device,
        device_id_type=MESH,
    ).start()


def drain(ref, sem):
    pltpu.make_async_copy(ref, ref, sem).wait()


def over(low, high, body):
    def step(index, carry):
        body(index)
        return carry

    lax.fori_loop(low, high, step, 0)


def iota(shape, dim):
    return lax.broadcasted_iota(jnp.int32, shape, dim)


def dot(a, b):
    return jnp.dot(a, b, preferred_element_type=F32)


def split3(value):
    high = value.astype(BF16).astype(F32)
    rest = value - high
    middle = rest.astype(BF16).astype(F32)
    return high, middle, rest - middle


def kernel_values(exponent):
    return jnp.exp2(exponent * (math.log2(math.e) / WIDTH)).astype(BF16)


def window_of(start):
    base = jnp.minimum(start // LANES, (ROWS - WINDOW) // LANES) * LANES
    return pl.multiple_of(base, LANES), start - base


MEM, MEM_REST, SIB, SIB_REST, TERM, FB, INV, SP, SPR, SR, SD, SH, SX, SC = (
    0, 1, 2, 3, 4, 5, 6, 7, 8, 10, 14, 18, 22, 26,
)
N_SEM = 30


def main_kernel(
    ft, wt, labels, inv, order, block_starts, out,
    fa, wv, wn, wide, picks, iv, a, mem, fb, o, term_send, acc, p, m,
    got_p, r0, r_send, r_full, d_part, d_got, d_own, h_own, h_full, c_part, c_got, high, low,
    send, recv, load,
):
    y = lax.axis_index("sy")
    x = lax.axis_index("sx")
    c = lax.axis_index("sc")
    z = lax.axis_index("cols")
    chip = y * 4 + x
    shard = chip * 2 + c
    sib = (y, x, 1 - c, z)
    scale = 1.0 / math.sqrt(ROWS * 32)

    def peer(offset):
        row = lax.rem(y + offset // 4, 4)
        col = lax.rem(x + lax.rem(offset, 4), 4)
        return row, col, row * 4 + col

    loads = [
        pltpu.make_async_copy(ft, fa.at[pl.ds(0, WIDTH)], load.at[0]),
        pltpu.make_async_copy(wt, wv, load.at[1]),
        pltpu.make_async_copy(inv, iv.at[c], load.at[2]),
    ]
    for copy in loads:
        copy.start()

    barrier = pltpu.get_barrier_semaphore()

    def greet_plane(offset):
        row, col, _ = peer(offset)
        pl.semaphore_signal(barrier, inc=1, device_id=(row, col, c, z), device_id_type=MESH)

    def greet_column(offset):
        other = lax.rem(z + offset, COLS)
        pl.semaphore_signal(barrier, inc=1, device_id=(y, x, c, other), device_id_type=MESH)

    pl.semaphore_signal(barrier, inc=1, device_id=sib, device_id_type=MESH)
    over(1, CHIPS, greet_plane)
    over(1, COLS, greet_column)

    starts = []
    for t in range(UPD):
        start = jnp.int32(0)
        for block in range(BLOCKS):
            start += jnp.where(order[t] == block, block_starts[block], 0)
        starts.append(start)

    column = iota((1, LANES), 1)
    target = jnp.full((1, LANES), -1, jnp.int32)
    for t in range(UPD):
        here = column // PIECE == t
        target = jnp.where(here, starts[t] + z * PIECE + lax.rem(column, PIECE), target)
    picks[...] = (iota((ROWS, LANES), 0) == target).astype(BF16)
    loads[0].wait()
    chosen = dot(fa[0:WIDTH, :], picks[...])
    norm = jnp.sum(jnp.square(chosen), axis=0, keepdims=True)
    line = iota((8, LANES), 0)
    extra = jnp.where(line < 6, 1.0, 0.0)
    for number, part in enumerate(split3(norm)):
        extra = jnp.where(line == number + 3, -part, extra)
    rest = jnp.zeros((DEPTH - WIDTH - 8, LANES), F32)
    chosen = jnp.concatenate([2.0 * chosen, extra, rest], axis=0).T.astype(BF16)
    for t in range(UPD):
        mem[t] = chosen[t * PIECE : (t + 1) * PIECE]

    pl.semaphore_wait(barrier, 1 + 15 + 7)

    def send_members(first, count, number):
        def body(offset):
            row, col, _ = peer(offset)
            push(
                mem.at[pl.ds(first, count)],
                a.at[pl.ds(first, count), chip, c],
                send.at[number],
                recv.at[number],
                (row, col, c, z),
            )

        over(1, CHIPS, body)
        for t in range(first, first + count):
            a[t, chip, c] = mem[t]

    def forward_members(first, count, number, onward):
        drain(a.at[pl.ds(first, count), pl.ds(0, 15), 0], recv.at[number])
        ours = a.at[pl.ds(first, count), :, c]
        push(ours, ours, send.at[onward], recv.at[onward], sib)

    send_members(0, 1, MEM)
    send_members(1, 3, MEM_REST)

    line = iota((8, NBLOCK), 0)
    for block in range(ROWS // NBLOCK):
        cols = pl.ds(block * NBLOCK, NBLOCK)
        norm = jnp.sum(jnp.square(fa[0:WIDTH, cols].astype(F32)), axis=0, keepdims=True)
        extra = jnp.where(line < 6, 1.0, 0.0)
        for number, part in enumerate(split3(norm)):
            extra = jnp.where(line == number, -part, extra)
        tail = fa[432:440, cols].astype(F32)
        fa[432:448, cols] = jnp.concatenate([tail, extra], axis=0).astype(BF16)
        fa[448:DEPTH, cols] = jnp.zeros((DEPTH - 448, NBLOCK), BF16)

    loads[1].wait()
    values = [dot(part.astype(BF16), picks[...]) for part in split3(wv[...])]
    values = values[0] + values[1] + values[2]
    known = dot(jnp.broadcast_to(labels[...].astype(F32), (8, ROWS)).astype(BF16), picks[...])
    onehot = (iota((CLASSES, LANES), 0).astype(F32) == known[0:1]).astype(F32)
    wide[...] = jnp.zeros_like(wide)
    wide[0:CLASSES, :] = onehot - RIDGE * values
    terms = wide[...].T
    for t in range(UPD):
        first = terms[t * PIECE : (t + 1) * PIECE, 0:LANES]
        second = terms[t * PIECE : (t + 1) * PIECE, LANES:]
        o[t, c] = jnp.where(c == 0, first, second)
        term_send[t] = jnp.where(c == 0, second, first)
    push(term_send, o.at[:, c], send.at[TERM], recv.at[TERM], sib)
    for t in range(UPD - 1):
        picks[...] = (iota((ROWS, SPAN), 0) == starts[t] + iota((1, SPAN), 1)).astype(BF16)
        fb[c, t] = dot(fa[...], picks[...]).astype(BF16)
    push(fb.at[c], fb.at[c], send.at[FB], recv.at[FB], sib)
    push(inv, iv.at[c], send.at[INV], recv.at[INV], sib)
    for block in range(ROWS // NBLOCK):
        cols = pl.ds(block * NBLOCK, NBLOCK)
        wn[cols, :] = jnp.zeros((NBLOCK, 2 * LANES), BF16)
        wn[cols, 0:CLASSES] = wv[:, cols].T.astype(BF16)

    def panel(t, first, last):
        def body(block):
            cols = pl.ds(pl.multiple_of(block * NBLOCK, NBLOCK), NBLOCK)
            for half in range(2):
                rows = pl.ds(half * 256, 256)
                lines = a[t, pl.ds(half * 8, 8)].reshape(256, DEPTH)
                values = kernel_values(dot(lines, fa[:, cols]))
                acc[rows, :] += dot(values, wn[cols, :])

        if first == 0:
            acc[...] = jnp.zeros_like(acc)
        over(first, last, body)
        if last == ROWS // NBLOCK:
            for half in range(2):
                part = acc[:, half * LANES : (half + 1) * LANES].astype(BF16)
                p[half, t] = part.reshape(CHIPS, 32, LANES)

    def margin(early, late):
        lines = a[late].reshape(GROUP, DEPTH)
        for half in range(2):
            m[EARLIER.index((early, late)), half] = kernel_values(dot(lines, fb[half, early]))

    def send_products(first, count, number):
        def body(offset):
            row, col, other = peer(offset)
            for core in range(2):

                @pl.when((offset > 0) | (core != c))
                def _():
                    push(
                        p.at[core, pl.ds(first, count), other],
                        got_p.at[pl.ds(first, count), shard],
                        send.at[number],
                        recv.at[number],
                        (row, col, core, z),
                    )

        over(0, CHIPS, body)

    def sums_of_products(first, count, number):
        drain(got_p.at[pl.ds(first, count), pl.ds(0, 31)], recv.at[number])
        for t in range(first, first + count):
            got_p[t, shard] = p[c, t, chip]
            own = o[t].reshape(32, LANES)
            r0[t] = own - scale * jnp.sum(got_p[t].astype(F32), axis=0)

    def send_residual(t):
        def body(offset):
            row, col, _ = peer(offset)
            push(r_send.at[t], r_full.at[t, chip], send.at[SR + t], recv.at[SR + t], (row, col, c, z))

        over(1, CHIPS, body)
        r_full[t, chip] = r_send[t]

    def split_inverse(t):
        for half in range(2):
            value = iv[half, t]
            top = value.astype(BF16)
            high[t, half] = top
            low[t, half] = (value - top.astype(F32)).astype(BF16)

    def partial_delta(t):
        drain(r_full.at[t, pl.ds(0, 15)], recv.at[SR + t])
        residual = r_full[t].reshape(GROUP, LANES)
        top = residual.astype(BF16)
        rest = (residual - top.astype(F32)).astype(BF16)
        for half in range(2):
            value = dot(high[t, half], top) + dot(high[t, half], rest) + dot(low[t, half], top)
            d_part[t, pl.ds(half * 4, 4)] = value.reshape(4, 32, LANES)

        def body(offset):
            other = lax.rem(z + offset, COLS)
            push(d_part.at[t, other], d_got.at[t, z], send.at[SD + t], recv.at[SD + t], (y, x, c, other))

        over(1, COLS, body)
        d_got[t, z] = d_part[t, z]

    keeper = z // 4
    place = pl.ds(pl.multiple_of(lax.rem(z, 4) * 32, 32), 32)

    def finish_delta(t):
        drain(d_got.at[t, pl.ds(0, 7)], recv.at[SD + t])
        delta = jnp.sum(d_got[t], axis=0)
        d_own[t] = delta
        if t < UPD - 1:
            h_own[t] = delta.astype(BF16)

            def send_high(offset):
                other = lax.rem(z + offset, COLS)
                push(h_own.at[t], h_full.at[t, z], send.at[SH + t], recv.at[SH + t], (y, x, c, other))

            over(1, COLS, send_high)
            h_full[t, z] = h_own[t]

        def send_result(offset):
            other = lax.rem(z + offset, COLS)

            @pl.when((offset > 0) | (keeper != c))
            def _():
                push(
                    d_own.at[t], out.at[t, c, place], send.at[SX + t], recv.at[SX + t],
                    (y, x, keeper, other),
                )

        over(0, COLS, send_result)

        @pl.when(keeper == c)
        def _():
            out[t, c, place] = d_own[t]

    def corrections(early, late):
        total = None
        for half in range(2):
            lines = h_full[early, pl.ds(half * 4, 4)].reshape(SPAN, LANES)
            part = dot(m[EARLIER.index((early, late)), half], lines)
            total = part if total is None else total + part
        return total

    def send_correction(t, partial):
        late = t + 1
        drain(h_full.at[t, pl.ds(0, 7)], recv.at[SH + t])
        part = corrections(t, late)
        partial = part if partial is None else partial + part
        c_part[t] = partial.astype(BF16).reshape(CHIPS, 32, LANES)

        def body(offset):
            row, col, other = peer(offset)
            push(
                c_part.at[t, other], c_got.at[t, chip], send.at[SC + t], recv.at[SC + t], (row, col, c, z)
            )

        over(1, CHIPS, body)
        c_got[t, chip] = c_part[t, chip]

    def next_residual(t):
        late = t + 1
        line = iota((32, 2 * SPAN), 0)
        column = iota((32, 2 * SPAN), 1)
        member = starts[late] + z * PIECE + lax.rem(line, PIECE)
        same = line // PIECE == column // SPAN
        shared = jnp.zeros((32, LANES), F32)
        for early in range(late):
            hit = same & (member == starts[early] + lax.rem(column, SPAN))
            shared += dot(
                jnp.where(hit, RIDGE, 0.0).astype(BF16), h_full[early].reshape(2 * SPAN, LANES)
            )
        drain(c_got.at[t, pl.ds(0, 15)], recv.at[SC + t])
        r_send[late] = r0[late] - shared - scale * jnp.sum(c_got[t].astype(F32), axis=0)
        send_residual(late)

    whole = ROWS // NBLOCK
    forward_members(0, 1, MEM, SIB)
    loads[2].wait()
    drain(a.at[pl.ds(0, 1), :, 1 - c], recv.at[SIB])
    panel(0, 0, whole)
    send_products(0, 1, SP)
    forward_members(1, 3, MEM_REST, SIB_REST)
    drain(iv.at[1 - c], recv.at[INV])
    split_inverse(1)
    drain(fb.at[1 - c], recv.at[FB])
    drain(o.at[:, 1 - c], recv.at[TERM])
    drain(a.at[pl.ds(1, 3), :, 1 - c], recv.at[SIB_REST])
    split_inverse(0)
    panel(1, 0, whole)
    sums_of_products(0, 1, SP)
    r_send[0] = r0[0]
    send_residual(0)
    panel(2, 0, whole)
    partial_delta(0)
    send_products(1, 2, SPR)
    panel(3, 0, whole)
    finish_delta(0)
    send_products(3, 1, SPR + 1)
    margin(0, 1)
    send_correction(0, None)
    sums_of_products(1, 2, SPR)
    next_residual(0)
    partial_delta(1)
    margin(0, 2)
    margin(0, 3)
    partial = corrections(0, 2)
    finish_delta(1)
    margin(1, 2)
    margin(1, 3)
    send_correction(1, partial)
    sums_of_products(3, 1, SPR + 1)
    next_residual(1)
    split_inverse(2)
    partial_delta(2)
    partial = corrections(0, 3) + corrections(1, 3)
    finish_delta(2)
    margin(2, 3)
    send_correction(2, partial)
    split_inverse(3)
    next_residual(2)
    partial_delta(3)
    finish_delta(3)

    for t in range(UPD):

        @pl.when(keeper == c)
        def _():
            drain(d_got.at[t, pl.ds(0, 7)], recv.at[SX + t])
            drain(d_got.at[t, pl.ds(0, 7)], send.at[SX + t])

        @pl.when(keeper != c)
        def _():
            drain(d_got.at[t], recv.at[SX + t])
            drain(d_got.at[t], send.at[SX + t])

        drain(r_full.at[t, pl.ds(0, 15)], send.at[SR + t])
        drain(d_got.at[t, pl.ds(0, 7)], send.at[SD + t])
        if t < UPD - 1:
            drain(h_full.at[t, pl.ds(0, 7)], send.at[SH + t])
            drain(c_got.at[t, pl.ds(0, 15)], send.at[SC + t])
    drain(got_p.at[pl.ds(0, 1), pl.ds(0, 31)], send.at[SP])
    drain(got_p.at[pl.ds(0, 2), pl.ds(0, 31)], send.at[SPR])
    drain(got_p.at[pl.ds(0, 1), pl.ds(0, 31)], send.at[SPR + 1])
    drain(a.at[pl.ds(0, 1), pl.ds(0, 15), 0], send.at[MEM])
    drain(a.at[pl.ds(1, 3), pl.ds(0, 15), 0], send.at[MEM_REST])
    drain(a.at[pl.ds(0, 1), :, 0], send.at[SIB])
    drain(a.at[pl.ds(1, 3), :, 0], send.at[SIB_REST])
    drain(fb.at[0], send.at[FB])
    drain(iv.at[0], send.at[INV])
    drain(term_send, send.at[TERM])


def deltas_of(ft, wt, labels, inv, order, starts):
    vmem = pltpu.VMEM
    return pl.pallas_call(
        main_kernel,
        out_shape=jax.ShapeDtypeStruct((UPD, 2, SPAN, LANES), F32),
        in_specs=[ANY, ANY, VMEM, ANY, SMEM, SMEM],
        out_specs=VMEM,
        scratch_shapes=[
            vmem((DEPTH, ROWS), BF16),
            vmem((CLASSES, ROWS), F32),
            vmem((ROWS, 2 * LANES), BF16),
            vmem((2 * LANES, LANES), F32),
            vmem((ROWS, LANES), BF16),
            vmem((2, UPD, SPAN, GROUP), F32),
            vmem((UPD, CHIPS, 2, PIECE, DEPTH), BF16),
            vmem((UPD, PIECE, DEPTH), BF16),
            vmem((2, UPD - 1, DEPTH, SPAN), BF16),
            vmem((UPD, 2, PIECE, LANES), F32),
            vmem((UPD, PIECE, LANES), F32),
            vmem((GROUP, 2 * LANES), F32),
            vmem((2, UPD, CHIPS, 32, LANES), BF16),
            vmem((len(EARLIER), 2, GROUP, SPAN), BF16),
            vmem((UPD, 2 * CHIPS, 32, LANES), BF16),
            vmem((UPD, 32, LANES), F32),
            vmem((UPD, 32, LANES), F32),
            vmem((UPD, CHIPS, 32, LANES), F32),
            vmem((UPD, COLS, 32, LANES), F32),
            vmem((UPD, COLS, 32, LANES), F32),
            vmem((UPD, 32, LANES), F32),
            vmem((UPD - 1, 32, LANES), BF16),
            vmem((UPD - 1, COLS, 32, LANES), BF16),
            vmem((UPD - 1, CHIPS, 32, LANES), BF16),
            vmem((UPD - 1, CHIPS, 32, LANES), BF16),
            vmem((UPD, 2, SPAN, GROUP), BF16),
            vmem((UPD, 2, SPAN, GROUP), BF16),
            pltpu.SemaphoreType.DMA((N_SEM,)),
            pltpu.SemaphoreType.DMA((N_SEM,)),
            pltpu.SemaphoreType.DMA((3,)),
        ],
        compiler_params=pltpu.CompilerParams(
            collective_id=0, has_side_effects=True, vmem_limit_bytes=64 << 20
        ),
        name="updates",
    )(ft, wt, labels, inv, order, starts)


def add_kernel(wt, deltas, order, block_starts, out):
    out[...] = wt[...]
    for t in range(UPD):
        base, shift = window_of(block_starts[order[t]])
        rows = jnp.concatenate([deltas[t, 0].T, deltas[t, 1].T], axis=0)[:CLASSES]
        wide = jnp.concatenate([rows, jnp.zeros((CLASSES, WINDOW - SPAN), F32)], axis=1)
        out[:, pl.ds(base, WINDOW)] += pltpu.roll(wide, shift, 1)


def add_deltas(wt, deltas, order, starts):
    return pl.pallas_call(
        add_kernel,
        out_shape=jax.ShapeDtypeStruct(wt.shape, wt.dtype),
        in_specs=[VMEM, VMEM, SMEM, SMEM],
        out_specs=VMEM,
        compiler_params=pltpu.CompilerParams(vmem_limit_bytes=64 << 20),
        name="add_deltas",
    )(wt, deltas, order, starts)


def local(features, labels, weights, block_order, block_starts, inverses):
    wt = weights.T
    deltas = deltas_of(
        features.T, wt, labels.reshape(1, ROWS), inverses, block_order, block_starts
    )
    return add_deltas(wt, deltas, block_order, block_starts).T


def solution(mesh):
    finer = Mesh(
        mesh.devices.reshape(4, 4, 2, mesh.shape["cols"]), ("sy", "sx", "sc", "cols")
    )
    in_specs = (P(SAMPLES, None), P(SAMPLES), P(SAMPLES, None), P(), P(), P(None, SAMPLES, "cols"))
    return jax.shard_map(
        local, mesh=finer, in_specs=in_specs, out_specs=P(SAMPLES, None), check_vma=False
    )
```
